32 devices in a mesh: lon: 8 (over y, x, core), lat: 4 (over z).
Axes of the slice: x: 2, y: 2, z: 4, core: 2. Of those that a mesh axis runs over, the one named last changes fastest.
Arguments:
- tracers: float32 [2, 8, 192, 1024], P(None, None, 'lat', 'lon'), may hold values from -6 to 6
- east_courant: float32 [8, 192, 1024], P(None, 'lat', 'lon'), may hold values from -0.25 to 0.25
- north_courant: float32 [8, 192, 1024], P(None, 'lat', 'lon'), may hold values from -0.25 to 0.25
- diffusivity: float32 [8, 192, 1024], P(None, 'lat', 'lon'), may hold values from 0.01 to 0.12
- wet_levels: int32 [192, 1024], P('lat', 'lon'), may hold values from 0 to 8
Outputs:
- advected: float32 [2, 8, 192, 1024], P(None, None, 'lat', 'lon')
The draws below stay inside these ranges and needn't reach their ends.
All inputs are finite; a program needn't handle non-finite values.
Results may differ from the reference program's by a relative error of at most 0.0003.
Values sent between devices are 32-bit elements; how exact they have to be, the bound alone decides.
No kernel may reach another device: no remote copies, remote signals or barrier semaphores. Data moves between devices by JAX's collectives and lax.ppermute only.
A program may use at most 64 MiB of HBM per device.

```python
import math
import jax
import jax.numpy as jnp

LEV = 8
STEPS = 3
NLON = 1024
NLAT = 192


def set_ends(entries, key, least, largest):
    dims = entries.shape
    index_at = [jax.random.randint(jax.random.fold_in(key, axis), (), 0, dims[axis]) for axis in range(len(dims))]
    entries = entries.at[tuple(index_at)].set(least)
    longest = dims.index(max(dims))
    index_at[longest] = (index_at[longest] + 1) % dims[longest]
    return entries.at[tuple(index_at)].set(largest)


def steps_of(own_key, shape, pieces, least, largest):
    def one(axis_at, shards_of):
        draws = jax.random.uniform(jax.random.fold_in(jax.random.fold_in(own_key, 6), axis_at), (shards_of,), jnp.float32, least / len(pieces), largest / len(pieces))
        return jnp.repeat(jnp.exp(draws), shape[axis_at] // shards_of).reshape((-1,) + (1,) * (len(shape) - axis_at - 1))

    loudness = one(*pieces[0])
    for cut in pieces[1:]:
        loudness = loudness * one(*cut)
    return loudness


def normal_values(own_key, extent, spread, limit, split=(), kind=jnp.bfloat16):
    level = steps_of(own_key, extent, split, -0.22, 0.18) if split else 1.0
    result = jax.random.normal(own_key, extent, jnp.float32) * spread * level
    return jnp.minimum(jnp.maximum(result, -limit), limit).astype(kind)


def setup_inputs(seed: int = 0) -> dict:
    splits = jax.random.split(jax.random.key(seed), 6)
    tracers = normal_values(splits[0], (2, LEV, NLAT, NLON), 1.0, 6.0, ((2, 4), (3, 8)), jnp.float32)
    east_courant = jnp.clip(jax.random.uniform(splits[1], (LEV, NLAT, NLON), jnp.float32, -0.25, 0.25) * steps_of(splits[1], (LEV, NLAT, NLON), ((1, 4), (2, 8)), -0.4, 0.0), -0.25, 0.25)
    north_courant = jnp.clip(jax.random.uniform(splits[2], (LEV, NLAT, NLON), jnp.float32, -0.25, 0.25) * steps_of(splits[2], (LEV, NLAT, NLON), ((1, 4), (2, 8)), -0.4, 0.0), -0.25, 0.25)
    diffusivity = jnp.clip(jnp.exp(math.log(0.12) - 2.4849066 * jax.random.uniform(splits[3], (LEV, NLAT, NLON), jnp.float32) ** steps_of(splits[3], (LEV, NLAT, NLON), ((1, 4), (2, 8)), -0.2, 0.2)), 0.01, 0.12)
    wet_levels = set_ends(jax.random.randint(splits[4], (NLAT, NLON), 0, LEV + 1), jax.random.fold_in(splits[4], 1), 0, LEV).astype(jnp.int32)
    return dict(tracers=tracers, east_courant=east_courant, north_courant=north_courant, diffusivity=diffusivity, wet_levels=wet_levels)


def minmod(first, second):
    return 0.5 * (jnp.sign(first) + jnp.sign(second)) * jnp.minimum(jnp.abs(first), jnp.abs(second))


def face_flux(behind, left_cell, right_cell, beyond, courant, face_kappa, face_mask):
    difference = right_cell - left_cell
    forward = courant > 0
    upwind = jnp.where(forward, left_cell, right_cell)
    upslope = jnp.where(forward, left_cell - behind, beyond - right_cell)
    magnitude = jnp.abs(courant)
    limited = minmod(difference, upslope)
    return (courant * upwind + 0.5 * magnitude * (1.0 - magnitude) * limited - face_kappa * difference) * face_mask


def reference(tracers, east_courant, north_courant, diffusivity, wet_levels):
    layers = jnp.arange(LEV, dtype=jnp.int32)[:, None, None]
    wetness = (layers < wet_levels[None]).astype(jnp.float32)
    east_kappa = 0.5 * (diffusivity + jnp.roll(diffusivity, -1, 2))
    east_mask = wetness * jnp.roll(wetness, -1, 2)
    fold_speed = 0.5 * (north_courant[:, -1] - north_courant[:, -1, ::-1])
    empty_row = jnp.zeros((LEV, 1, NLON), jnp.float32)
    north_speed = jnp.concatenate([empty_row, north_courant[:, :NLAT - 1], fold_speed[:, None]], 1)
    kappa_rows = jnp.concatenate([empty_row, diffusivity, diffusivity[:, -1:, ::-1]], 1)
    wet_rows = jnp.concatenate([empty_row, wetness, wetness[:, -1:, ::-1]], 1)
    north_kappa = 0.5 * (kappa_rows[:, :-1] + kappa_rows[:, 1:])
    north_mask = wet_rows[:, :-1] * wet_rows[:, 1:]
    face_count = NLAT + 1
    current = tracers
    for repeat in range(STEPS):
        east_flux = face_flux(jnp.roll(current, 1, 3), current, jnp.roll(current, -1, 3), jnp.roll(current, -2, 3), east_courant, east_kappa, east_mask)
        extended = jnp.concatenate([jnp.zeros((2, LEV, 2, NLON), jnp.float32), current, current[:, :, -1:, ::-1], current[:, :, -2:-1, ::-1]], 2)
        north_flux = face_flux(extended[:, :, 0:face_count], extended[:, :, 1:face_count + 1], extended[:, :, 2:face_count + 2], extended[:, :, 3:face_count + 3], north_speed, north_kappa, north_mask)
        current = current - (east_flux - jnp.roll(east_flux, 1, 3)) - (north_flux[:, :, 1:] - north_flux[:, :, :-1])
    return current
```

```python
import jax
import jax.numpy as jnp
from jax import lax
from jax.experimental import pallas as pl
from jax.experimental.pallas import tpu as pltpu
from jax.sharding import PartitionSpec as P

STEPS = 3
HALO = 2 * STEPS
AXES = ("lon", "lat")
GROUP = 4
PLANES = 5
SLOT = HALO
STRIP = 6 * HALO
VMEM = pl.BlockSpec(memory_space=pltpu.VMEM)

AT_T, AT_E, AT_N, AT_K, AT_WET, AT_PACK, AT_PACK_WET, MESSAGE = 0, 12, 16, 21, 26, 27, 31, 32
N_E, N_N, N_K = HALO - 2, HALO - 1, HALO - 1


def lanes(shape):
    return lax.broadcasted_iota(jnp.int32, shape, len(shape) - 1)


def levels_of(shape):
    return lax.broadcasted_iota(jnp.int32, shape, 0).astype(jnp.float32)


def take(value, index):
    return jnp.take_along_axis(value, index, axis=1)


def east_of(value):
    return pltpu.roll(value, value.shape[1] - 1, 1)


def west_of(value):
    return pltpu.roll(value, 1, 1)


def coefficients(speed, kappa, other_kappa, mask):
    speed = speed * mask
    magnitude = jnp.abs(speed)
    spread = jnp.minimum(speed, 0.0) - (0.5 * mask) * (kappa + other_kappa)
    return speed, spread, 0.5 * magnitude * (1.0 - magnitude)


def flux(cell, before, here, after, face):
    speed, spread, slope = face
    upslope = jnp.where(speed > 0, before, after)
    limited = jnp.maximum(
        jnp.minimum(here, upslope), jnp.minimum(jnp.maximum(here, upslope), 0.0)
    )
    return speed * cell + spread * here + slope * limited


def advance(low, high, cell_at, east_at, north_at, put):
    cells = {r: cell_at(r) for r in range(low - 2, low + 2)}
    slope = {r: cells[r + 1] - cells[r] for r in range(low - 2, low + 1)}
    below = flux(cells[low - 1], slope[low - 2], slope[low - 1], slope[low], north_at(low - 1))
    for r in range(low, high):
        cells[r + 2] = cell_at(r + 2)
        slope[r + 1] = cells[r + 2] - cells[r + 1]
        above = flux(cells[r], slope[r - 1], slope[r], slope[r + 1], north_at(r))
        step = east_of(cells[r]) - cells[r]
        eastern = flux(cells[r], west_of(step), step, east_of(step), east_at(r))
        put(r, cells[r] - (eastern - west_of(eastern)) - (above - below))
        below = above


def parities():
    lon_even = lax.rem(lax.axis_index("lon"), 2) == 0
    lat = lax.axis_index("lat")
    return lon_even, lax.rem(lat, 2) == 0, lat == lax.axis_size("lat") - 1


def wet_row(wet_ref, row):
    return wet_ref[pl.ds(row, 1), :].astype(jnp.float32)


def pack_kernel(tr, ec, nc, kd, wet, p0, p1, xm, ym):
    rows, cols = wet.shape
    lev = ec.shape[0] // rows
    lon_even, lat_even, _ = parities()
    lane = lanes((lev, cols))

    def plane(p, r):
        if p < 2:
            return tr[pl.ds(p * lev * rows + r, lev, stride=rows), :]
        return (ec, nc, kd)[p - 2][pl.ds(r, lev, stride=rows), :]

    def place(pair, value, slot):
        if pair is None:
            pair = (jnp.zeros_like(value), jnp.zeros_like(value))
        inside = (lane >= slot * SLOT) & (lane < slot * SLOT + SLOT)
        eastern = pltpu.roll(value, slot * SLOT + SLOT, 1)
        western = pltpu.roll(value, slot * SLOT, 1) if slot else value
        return jnp.where(inside, eastern, pair[0]), jnp.where(inside, western, pair[1])

    def emit(at, pair):
        p0[at] = jnp.where(lon_even, pair[0], pair[1])
        p1[at] = jnp.where(lon_even, pair[1], pair[0])

    for g in range(rows // GROUP):
        pair = None
        for k in range(GROUP):
            for p in range(PLANES):
                pair = place(pair, plane(p, g * GROUP + k), k * PLANES + p)
        emit(g, pair)
    pair = None
    for tile in range(rows // lev):
        pair = place(pair, wet[pl.ds(tile * lev, lev), :].astype(jnp.float32), tile)
    emit(rows // GROUP, pair)

    for out, north in ((xm, lat_even), (ym, jnp.logical_not(lat_even))):
        row = [jnp.where(north, rows - 1 - m, m) for m in range(HALO)]
        for m in range(HALO):
            for p in range(2):
                out[AT_T + 2 * m + p] = plane(p, row[m])
        for m in range(N_E):
            out[AT_E + m] = plane(2, row[m])
        for m in range(N_N):
            out[AT_N + m] = plane(3, row[m])
        for m in range(N_K):
            out[AT_K + m] = plane(4, row[m])
        out[AT_WET] = jnp.zeros((lev, cols), jnp.float32)
        for m in range(N_K):
            out[AT_WET, pl.ds(m, 1), :] = wet_row(wet, row[m])


def sides(lon_even, r0, r1, at):
    a, b = r0[at], r1[at]
    return jnp.where(lon_even, a, b), jnp.where(lon_even, b, a)


def forward_kernel(xm, ym, r0, r1, x, y):
    lev, cols = xm.shape[1:]
    groups = r0.shape[0] - 1
    tiles = groups * GROUP // lev
    lon_even, lat_even, _ = parities()
    lane = lanes((lev, cols))
    span = PLANES * SLOT
    turned = lane
    for k in range(GROUP):
        here = (lane >= k * span) & (lane < k * span + span)
        turned = jnp.where(here, lane + (GROUP - 1 - 2 * k) * span, turned)
    for part, out, north in ((xm, x, lat_even), (ym, y, jnp.logical_not(lat_even))):
        for i in range(AT_PACK):
            out[i] = part[i]
        index = jnp.where(north, turned, lane)
        for h in range(2):
            pair = sides(lon_even, r0, r1, jnp.where(north, groups - 1 - h, h))
            for s in range(2):
                out[AT_PACK + 2 * s + h] = take(pair[s], index)
        pair = sides(lon_even, r0, r1, groups)
        index = jnp.where(north, lane + (tiles - 1) * SLOT, lane)
        eastern = take(pair[0], jnp.minimum(index, cols - 1))
        western = pltpu.roll(take(pair[1], jnp.minimum(index, cols - 1)), SLOT, 1)
        out[AT_PACK_WET] = jnp.where(lane < SLOT, eastern, western)


def interior_kernel(tr, ec, nc, kd, wet, t0, t1, t2, t3, raw, face):
    rows, cols = wet.shape
    lev = ec.shape[0] // rows
    level = levels_of((lev, cols))

    def mask_at(r):
        return jnp.where(level < wet_row(wet, r), 1.0, 0.0)

    mask = mask_at(0)
    for r in range(rows):
        for p in range(2):
            t0[r, p] = tr[pl.ds(p * lev * rows + r, lev, stride=rows), :]
        for p, source in enumerate((ec, nc, kd)):
            raw[r, p] = source[pl.ds(r, lev, stride=rows), :]
        kappa = raw[r, 2]
        put_face(face, r, 0, coefficients(raw[r, 0], kappa, east_of(kappa), mask * east_of(mask)))
        if r + 1 < rows:
            higher = kd[pl.ds(r + 1, lev, stride=rows), :]
            mask_above = mask_at(r + 1)
            put_face(face, r, 3, coefficients(raw[r, 1], kappa, higher, mask * mask_above))
            mask = mask_above
    sources, results = (t0, t1, t2), (t1, t2, t3)
    for s in range(STEPS):
        for p in range(2):
            advance(
                2 * s + 2,
                rows - 2 * s - 2,
                lambda r: sources[s][r, p],
                lambda r: get_face(face, r, 0),
                lambda r: get_face(face, r, 3),
                lambda r, v: results[s].__setitem__((r, p), v),
            )


def put_face(face, r, at, values):
    for i in range(3):
        face[r, at + i] = values[i]


def get_face(face, r, at):
    return tuple(face[r, at + i] for i in range(3))


class Strip:
    def __init__(self, lev, cols):
        lane = lanes((lev, cols))
        self.half = cols // 2
        self.second = lane >= self.half
        q = jnp.where(self.second, lane - self.half, lane)
        self.base = lane - q
        self.q = q
        self.own = jnp.clip(
            jnp.where(q < 2 * HALO, q + cols - 2 * HALO, q - 4 * HALO), 0, cols - 1
        )
        self.is_east = (q >= 2 * HALO) & (q < 3 * HALO)
        self.is_west = (q >= 3 * HALO) & (q < 4 * HALO)
        self.offset = jnp.clip(jnp.where(q < 3 * HALO, q - 2 * HALO, q - 3 * HALO), 0, HALO - 1)
        self.lane = lane
        self.cols = cols

    def join(self, own, eastern, western):
        return jnp.where(self.is_east, eastern, jnp.where(self.is_west, western, own))

    def one(self, main, eastern, western, slot, west_shift=0):
        index = self.offset + slot * SLOT
        west_index = index + west_shift if west_shift else index
        return self.join(take(main, self.own), take(eastern, index), take(western, west_index))

    def both(self, first, second, eastern, western, slot):
        index = self.offset + jnp.where(self.second, slot * SLOT + SLOT, slot * SLOT)
        own = jnp.where(self.second, take(second, self.own), take(first, self.own))
        return self.join(own, take(eastern, index), take(western, index))

    def back(self, main, strip, p):
        index = jnp.where(self.lane < HALO, self.lane + 4 * HALO, self.lane - self.cols + 2 * HALO)
        index = jnp.clip(index, 0, STRIP - 1) + p * self.half
        edge = (self.lane < HALO) | (self.lane >= self.cols - HALO)
        return jnp.where(edge, take(strip, index), main)


def strip_kernel(t0, t3, raw, wet, r0, r1, out, s0, s1, s2, s3, face, ends):
    rows, cols = wet.shape
    lev = t0.shape[2]
    lon_even, _, _ = parities()
    strip = Strip(lev, cols)
    level = levels_of((lev, cols))
    groups = rows // GROUP
    wet_east, wet_west = r0, r1

    def mask_at(r):
        at = pl.ds(r % lev, 1)
        a = jnp.broadcast_to(r0[groups, at, :], (lev, cols))
        b = jnp.broadcast_to(r1[groups, at, :], (lev, cols))
        own = jnp.broadcast_to(wet_row(wet, r), (lev, cols))
        eastern, western = jnp.where(lon_even, a, b), jnp.where(lon_even, b, a)
        return jnp.where(level < strip.one(own, eastern, western, r // lev), 1.0, 0.0)

    def planes_at(r):
        pair = sides(lon_even, r0, r1, r // GROUP)
        slot = (r % GROUP) * PLANES
        s0[r] = strip.both(t0[r, 0], t0[r, 1], *pair, slot)
        return [strip.one(raw[r, i], *pair, slot + 2 + i) for i in range(3)] + [mask_at(r)]

    speed_e, speed_n, kappa, mask = planes_at(0)
    for r in range(rows):
        if r == 0 or r == rows - 1:
            for i, value in enumerate((speed_n, kappa, mask)):
                ends[r // (rows - 1), i] = value
        put_face(face, r, 0, coefficients(speed_e, kappa, east_of(kappa), mask * east_of(mask)))
        if r + 1 < rows:
            higher = planes_at(r + 1)
            put_face(face, r, 3, coefficients(speed_n, kappa, higher[2], mask * higher[3]))
            speed_e, speed_n, kappa, mask = higher
    sources, results = (s0, s1, s2), (s1, s2, s3)
    for s in range(STEPS):
        advance(
            2 * s + 2,
            rows - 2 * s - 2,
            lambda r: sources[s][r],
            lambda r: get_face(face, r, 0),
            lambda r: get_face(face, r, 3),
            lambda r, v: results[s].__setitem__(r, v),
        )
    for r in range(HALO, rows - HALO):
        for p in range(2):
            out[pl.ds(p * lev * rows + r, lev, stride=rows), :] = strip.back(t3[r, p], s3[r], p)


def frame_kernel(mid, t0, t1, t2, raw, face, wet, s0, s1, s2, sface, ends, x, y, out):
    rows, cols = wet.shape
    lev = t0.shape[2]
    _, lat_even, top = parities()
    strip = Strip(lev, cols)
    level = levels_of((lev, cols))
    turn = jnp.where(top, -1.0, 1.0)
    lane = strip.lane

    out[...] = mid[...]

    def halo(north):
        def piece(at):
            a, b = x[at], y[at]
            return jnp.where(lat_even, a, b) if north else jnp.where(lat_even, b, a)

        def wet_piece(at, sub):
            a = jnp.broadcast_to(x[at, pl.ds(sub, 1), :], (lev, cols))
            b = jnp.broadcast_to(y[at, pl.ds(sub, 1), :], (lev, cols))
            return jnp.where(lat_even, a, b) if north else jnp.where(lat_even, b, a)

        def pair(m):
            return piece(AT_PACK + m // GROUP), piece(AT_PACK + 2 + m // GROUP)

        main = dict(
            t=[[piece(AT_T + 2 * m + p) for p in range(2)] for m in range(HALO)],
            e=[piece(AT_E + m) for m in range(N_E)],
            n=[piece(AT_N + m) for m in range(N_N)],
            k=[piece(AT_K + m) for m in range(N_K)],
            w=[wet_piece(AT_WET, m) for m in range(N_K)],
        )
        slot = [(m % GROUP) * PLANES for m in range(HALO)]
        side = dict(
            t=[[strip.both(*main["t"][m], *pair(m), slot[m])] for m in range(HALO)],
            e=[strip.one(main["e"][m], *pair(m), slot[m] + 2) for m in range(N_E)],
            n=[strip.one(main["n"][m], *pair(m), slot[m] + 3) for m in range(N_N)],
            k=[strip.one(main["k"][m], *pair(m), slot[m] + 4) for m in range(N_K)],
            w=[],
        )
        for m in range(N_K):
            sub = jnp.where(top, lev - 1 - m, m) if north else lev - 1 - m
            corner = wet_piece(AT_PACK_WET, sub)
            side["w"].append(strip.one(main["w"][m], corner, corner, 0, SLOT))
        if north:
            cells = jnp.where(top, cols - 1 - lane, lane)
            faces = jnp.where(top, jnp.where(lane == cols - 1, cols - 1, cols - 2 - lane), lane)
            main = turned(main, cells, faces)
            last = STRIP - 1
            q = strip.q
            cells = jnp.where(top & (q <= last), strip.base + last - q, lane)
            faces = jnp.where(top & (q < last), strip.base + last - 1 - q, lane)
            side = turned(side, cells, faces)
        return main, side

    def turned(planes, cells, faces):
        return dict(
            t=[[take(v, cells) for v in values] for values in planes["t"]],
            e=[turn * take(v, faces) for v in planes["e"]],
            n=[turn * take(v, cells) for v in planes["n"]],
            k=[take(v, cells) for v in planes["k"]],
            w=[take(v, cells) for v in planes["w"]],
        )

    south, north = halo(False), halo(True)

    def run(kind, own, saved, own_face, end_planes):
        lower, upper = south[kind], north[kind]
        for planes in (lower, upper):
            planes["m"] = [jnp.where(level < w, 1.0, 0.0) for w in planes["w"]]
        (_, low_kappa, low_mask), (high_speed, high_kappa, high_mask) = end_planes
        east, northern = {}, {}
        for m in range(N_E):
            for r, planes in ((-1 - m, lower), (rows + m, upper)):
                kappa, mask = planes["k"][m], planes["m"][m]
                east[r] = coefficients(
                    planes["e"][m], kappa, east_of(kappa), mask * east_of(mask)
                )
        for m in range(N_N):
            kappa, mask = (low_kappa, low_mask) if m == 0 else (lower["k"][m - 1], lower["m"][m - 1])
            northern[-1 - m] = coefficients(
                lower["n"][m], lower["k"][m], kappa, lower["m"][m] * mask
            )
        for m in range(N_E + 1):
            if m == 0:
                kappa, mask = high_kappa, high_mask
                speed = jnp.where(top, 0.5 * (high_speed + upper["n"][0]), high_speed)
            else:
                kappa, mask = upper["k"][m - 1], upper["m"][m - 1]
                speed = jnp.where(top, upper["n"][m], upper["n"][m - 1]) if m < N_N else None
            northern[rows - 1 + m] = coefficients(speed, kappa, upper["k"][m], mask * upper["m"][m])
        east_at = lambda r: east[r] if r in east else get_face(own_face, r, 0)
        north_at = lambda r: northern[r] if r in northern else get_face(own_face, r, 3)
        finals = []
        for p in range(len(lower["t"][0])):
            now = {}
            for m in range(HALO):
                now[-1 - m], now[rows + m] = lower["t"][m][p], upper["t"][m][p]
            for s in range(STEPS):
                later = {}
                for low in (2 * s + 2 - HALO, rows - 2 * s - 2):
                    advance(
                        low,
                        low + HALO,
                        lambda r: now[r] if r in now else saved(s, r, p),
                        east_at,
                        north_at,
                        later.__setitem__,
                    )
                now = later
            finals.append(now)
        return finals

    def mask_at(r):
        return jnp.where(level < wet_row(wet, r), 1.0, 0.0)

    main_ends = [(raw[r, 1], raw[r, 2], mask_at(r)) for r in (0, rows - 1)]
    strip_ends = [tuple(ends[e, i] for i in range(3)) for e in range(2)]
    (columns,) = run(1, None, lambda s, r, p: (s0, s1, s2)[s][r], sface, strip_ends)
    finals = run(0, None, lambda s, r, p: (t0, t1, t2)[s][r, p], face, main_ends)
    for p in range(2):
        for r, value in finals[p].items():
            out[pl.ds(p * lev * rows + r, lev, stride=rows), :] = strip.back(value, columns[r], p)


def call(kernel, shapes, *operands, **options):
    return pl.pallas_call(
        kernel,
        out_shape=[jax.ShapeDtypeStruct(s, jnp.float32) for s in shapes],
        in_specs=[VMEM] * len(operands),
        out_specs=[VMEM] * len(shapes),
        **options,
    )(*operands)


def lon_swap(sizes, parity):
    lon, lat = sizes
    pairs = []
    for i in range(lon):
        other = (i + 1 if i % 2 == parity else i - 1) % lon
        pairs += [(i * lat + j, other * lat + j) for j in range(lat)]
    return pairs


def lat_swap(sizes, parity):
    lon, lat = sizes
    pairs = []
    for i in range(lon):
        for j in range(lat):
            if j % 2 != parity:
                if j > 0:
                    pairs.append((i * lat + j, i * lat + j - 1))
            elif j + 1 < lat:
                pairs.append((i * lat + j, i * lat + j + 1))
            else:
                pairs.append((i * lat + j, (lon - 1 - i) * lat + j))
    return pairs


def per_device(tracers, east_courant, north_courant, diffusivity, wet_levels):
    count, lev, rows, cols = tracers.shape
    sizes = (lax.axis_size("lon"), lax.axis_size("lat"))
    tr = tracers.reshape(count * lev * rows, cols)
    ec, nc, kd = (v.reshape(lev * rows, cols) for v in (east_courant, north_courant, diffusivity))
    block = (lev, cols)
    packed = (rows // GROUP + 1,) + block
    p0, p1, xm, ym = call(
        pack_kernel, [packed, packed, (AT_PACK,) + block, (AT_PACK,) + block],
        tr, ec, nc, kd, wet_levels,
    )
    r1 = lax.ppermute(p1, AXES, lon_swap(sizes, 1))
    r0 = lax.ppermute(p0, AXES, lon_swap(sizes, 0))
    state = (rows, count) + block
    t0, t1, t2, t3, raw, face = call(
        interior_kernel, [state] * 4 + [(rows, 3) + block, (rows, 6) + block],
        tr, ec, nc, kd, wet_levels,
    )
    x, y = call(forward_kernel, [(MESSAGE,) + block] * 2, xm, ym, r0, r1)
    y = lax.ppermute(y, AXES, lat_swap(sizes, 1))
    x = lax.ppermute(x, AXES, lat_swap(sizes, 0))
    mid, s0, s1, s2, s3, sface, ends = call(
        strip_kernel, [tr.shape] + [(rows,) + block] * 4 + [(rows, 6) + block, (2, 3) + block],
        t0, t3, raw, wet_levels, r0, r1,
    )
    (out,) = call(
        frame_kernel, [tr.shape],
        mid, t0, t1, t2, raw, face, wet_levels, s0, s1, s2, sface, ends, x, y,
    )
    return out.reshape(tracers.shape)


def solution(mesh):
    placed = (
        P(None, None, "lat", "lon"),
        P(None, "lat", "lon"),
        P(None, "lat", "lon"),
        P(None, "lat", "lon"),
        P("lat", "lon"),
    )
    return jax.shard_map(
        per_device,
        mesh=mesh,
        in_specs=placed,
        out_specs=P(None, None, "lat", "lon"),
        check_vma=False,
    )
```

```python
import jax
import jax.numpy as jnp
from jax import lax
from jax.experimental import pallas as pl
from jax.experimental.pallas import tpu as pltpu
from jax.sharding import PartitionSpec as P

STEPS = 3
HALO = 2 * STEPS
AXES = ("lon", "lat")
SUB = 8
PLANES = 5
KINDS = 3
PAIR = 2
SMALL = 16 << 20
VMEM = pl.BlockSpec(memory_space=pltpu.VMEM)
ANY = pl.BlockSpec(memory_space=pl.ANY)

AT_T, AT_E, AT_N, AT_K, AT_WET, MESSAGE = 0, 12, 16, 21, 26, 27
N_E, N_N, N_K = HALO - 2, HALO - 1, HALO - 1


def lanes(shape):
    return lax.broadcasted_iota(jnp.int32, shape, len(shape) - 1)


def take(value, index):
    return jnp.take_along_axis(value, index, axis=1)


def later_block(value):
    return pltpu.roll(value, value.shape[1] - 1, 1)


def earlier_block(value):
    return pltpu.roll(value, 1, 1)


def loop(count, body):
    def step(i, _):
        body(i)
        return 0

    lax.fori_loop(0, count, step, 0)


def parities():
    lon_even = lax.rem(lax.axis_index("lon"), 2) == 0
    lat = lax.axis_index("lat")
    return lon_even, lax.rem(lat, 2) == 0, lat == lax.axis_size("lat") - 1


def stage_kernel(tr, ec, nc, kd, wet, own, x, y, counts, done):
    lev = ec.shape[0]
    copies = [(tr, own.at[pl.ds(0, 2 * lev)]), (wet, counts)]
    copies += [(a, own.at[pl.ds(i * lev, lev)]) for i, a in ((2, ec), (3, nc), (4, kd))]
    copies = [pltpu.make_async_copy(a, b, done.at[i]) for i, (a, b) in enumerate(copies)]
    for copy in copies:
        copy.start()
    for copy in copies:
        copy.wait()
    own[own.shape[0] - 1] = counts[...].astype(jnp.float32)
    count, rows, cols = own.shape
    lev = count // PLANES
    _, lat_even, _ = parities()
    flat = own.reshape(count * rows, cols)
    for out, upper in ((x, lat_even), (y, jnp.logical_not(lat_even))):
        row = [jnp.where(upper, rows - 1 - m, m) for m in range(HALO)]

        def plane(i, m):
            return flat[pl.ds(i * lev * rows + row[m], lev, stride=rows), :]

        for m in range(HALO):
            for i in range(2):
                out[AT_T + 2 * m + i] = plane(i, m)
        for at, i, n in ((AT_E, 2, N_E), (AT_N, 3, N_N), (AT_K, 4, N_K)):
            for m in range(n):
                out[at + m] = plane(i, m)
        out[AT_WET] = jnp.zeros((lev, cols), jnp.float32)
        for m in range(N_K):
            out[AT_WET, pl.ds(m, 1), :] = own[count - 1, pl.ds(row[m], 1), :]


def turn_kernel(own, x, y, t0, se, sn, kw, p0, p1, te, ee, ne, ke):
    count, rows, cols = own.shape
    lev = count // PLANES
    planes = 2 * lev
    tall = rows + 2 * SUB
    lon_even, lat_even, top = parities()
    shape = (lev, cols)
    lane = lanes(shape)
    level = lax.broadcasted_iota(jnp.int32, shape, 0).astype(jnp.float32)
    zero = jnp.zeros((SUB, cols), jnp.float32)

    def fill(p):
        for e in range(tall // SUB):
            halo = e == 0 or e == tall // SUB - 1
            at = pl.ds(0 if halo else (e - 1) * SUB, SUB)

            def put_tile(target, q, value):
                target[pl.ds(pl.multiple_of(q * tall + e * SUB, SUB), SUB), :] = zero if halo else value

            for i in range(2):
                put_tile(te, p + i * lev, own[p + i * lev, at, :])
            put_tile(ee, p, own[p + 2 * lev, at, :])
            put_tile(ne, p, own[p + 3 * lev, at, :])
            counts = own[count - 1, at, :]
            put_tile(ke, p, jnp.where(counts > p.astype(jnp.float32), own[p + 4 * lev, at, :], -1.0))

    loop(lev, fill)

    turn = jnp.where(top, -1.0, 1.0)
    cells = jnp.where(top, cols - 1 - lane, lane)
    faces = jnp.where(top, jnp.where(lane == cols - 1, cols - 1, cols - 2 - lane), lane)
    for north in (False, True):
        def piece(at):
            a, b = x[at], y[at]
            return jnp.where(lat_even, a, b) if north else jnp.where(lat_even, b, a)

        def put(target, row, value, first=0):
            target[pl.ds(first * tall + row, lev, stride=tall), :] = value

        def turned(value, index):
            return take(value, index) if north else value

        at = [tall - SUB + m if north else SUB - 1 - m for m in range(HALO)]
        for m in range(HALO):
            for i in range(2):
                put(te, at[m], turned(piece(AT_T + 2 * m + i), cells), i * lev)
        wets = piece(AT_WET)
        for m in range(N_K):
            counts = jnp.broadcast_to(wets[m : m + 1], shape)
            kappa = jnp.where(level < counts, piece(AT_K + m), -1.0)
            put(ke, at[m], turned(kappa, cells))
        for m in range(N_E):
            value = turned(piece(AT_E + m), faces)
            put(ee, at[m], turn * value if north else value)
        if north:
            speeds = [turn * take(piece(AT_N + m), cells) for m in range(N_N)]
            last = ne[pl.ds(tall - SUB - 1, lev, stride=tall), :]
            put(ne, tall - SUB - 1, jnp.where(top, 0.5 * (last + speeds[0]), last))
            for m in range(N_E):
                put(ne, at[m], jnp.where(top, speeds[m + 1], speeds[m]))
        else:
            for m in range(N_N):
                put(ne, at[m], piece(AT_N + m))

    def transpose(i):
        for j in (2 * i, 2 * i + 1):
            for source, target, n in ((te, t0, planes), (ee, se, lev), (ne, sn, lev), (ke, kw, lev)):
                parts = [source[pl.ds(p * tall + j, tall // SUB, stride=SUB), :] for p in range(n)]
                matrix = jnp.concatenate(parts * (planes // n), 0)
                target[j, pl.ds(SUB, cols), :] = matrix.T

    loop(SUB // 2, transpose)
    for j in range(SUB):
        se[j, pl.ds(SUB - 1, 1), :] = se[j, pl.ds(SUB + cols - 1, 1), :]

    left = lanes((SUB, cols)) < cols // 2

    def edges(j):
        for out, eastern in ((p0, lon_even), (p1, jnp.logical_not(lon_even))):
            start = jnp.where(eastern, SUB + cols - HALO, SUB)
            here = pl.ds(start, SUB)
            faced = pl.ds(jnp.where(eastern, start, start - 1), SUB)
            kappa = kw[j, here, :]
            values = (
                t0[j, here, :],
                jnp.where(left, se[j, faced, :], sn[j, here, :]),
                jnp.where(left, jnp.maximum(kappa, 0.0), jnp.where(kappa > 0, 1.0, 0.0)),
            )
            for i, value in enumerate(values):
                out[pl.ds((KINDS * j + i) * HALO + 2, SUB), :] = value

    for out in (p0, p1):
        out[0:SUB, :] = zero
        out[out.shape[0] - SUB : out.shape[0], :] = zero
    loop(SUB, edges)


def coefficients(speed, kappa, other_kappa):
    wet = jnp.minimum(kappa, other_kappa) > 0
    speed = jnp.where(wet, speed, 0.0)
    magnitude = jnp.abs(speed)
    spread = jnp.minimum(speed, 0.0) - jnp.where(wet, 0.5 * (kappa + other_kappa), 0.0)
    return speed, spread, 0.5 * magnitude * (1.0 - magnitude)


def all_coefficients(se, sn, kw, face, low, at, kappa_low, kappa_high, north_low):
    here = pl.ds(at, SUB)
    kappa = [kw[j, here, :] for j in range(SUB)] + [kappa_high]
    for c, value in enumerate(coefficients(north_low, kappa_low, kappa[0])):
        low[c, here, :] = value
    for j in range(SUB):
        eastern = coefficients(se[j, here, :], kappa[j], kw[j, pl.ds(at + 1, SUB), :])
        northern = coefficients(sn[j, here, :], kappa[j], kappa[j + 1])
        for c, value in enumerate(eastern + northern):
            face[c, j, here, :] = value


def flux(cell, before, here, after, face):
    speed, spread, slope = face
    upslope = jnp.where(speed > 0, before, after)
    limited = jnp.maximum(
        jnp.minimum(here, upslope), jnp.minimum(jnp.maximum(here, upslope), 0.0)
    )
    return speed * cell + spread * here + slope * limited


def east_flux(t, face, s, j, at):
    behind, cell, after, beyond = (t[s, j, pl.ds(at + i, SUB), :] for i in (-1, 0, 1, 2))
    coefs = tuple(face[c, j, pl.ds(at, SUB), :] for c in range(3))
    return flux(cell, cell - behind, after - cell, beyond - after, coefs)


def advance(t, face, low, s, at, beside, fluxes=None):
    here = pl.ds(at, SUB)
    cell = [t[s, j, here, :] for j in range(SUB)]
    if fluxes is None:
        divergence = [
            east_flux(t, face, s, j, at) - east_flux(t, face, s, j, at - 1) for j in range(SUB)
        ]
    else:
        east = [east_flux(t, face, s, j, at) for j in range(SUB)]
        for j in range(SUB):
            fluxes[j, here, :] = east[j]
        divergence = [east[j] - fluxes[j, pl.ds(at - 1, SUB), :] for j in range(SUB)]
    rows = [beside[0], beside[1], *cell, beside[2], beside[3]]
    slope = [b - a for a, b in zip(rows, rows[1:])]
    north = []
    for j in range(-1, SUB):
        coefs = tuple(low[c, here, :] if j < 0 else face[3 + c, j, here, :] for c in range(3))
        north.append(flux(rows[j + 2], slope[j + 1], slope[j + 2], slope[j + 3], coefs))
    for j in range(SUB):
        t[s + 1, j, here, :] = cell[j] - divergence[j] - (north[j + 1] - north[j])


def rows_beside(t, s, at):
    here = pl.ds(at, SUB)
    before = [earlier_block(t[s, j, here, :]) for j in (SUB - 2, SUB - 1)]
    return before + [later_block(t[s, j, here, :]) for j in (0, 1)]


def interior_kernel(t0, se, sn, kw, t, face, low, fluxes, beside):
    cols = t.shape[3]
    passes = cols // SUB // PAIR

    def start(g):
        return pl.multiple_of(SUB + g * SUB, SUB)

    def turn_coefficients(b):
        values = []
        for k in range(PAIR):
            here = pl.ds(start(b * PAIR + k), SUB)
            values.append((
                earlier_block(kw[SUB - 1, here, :]),
                later_block(kw[0, here, :]),
                earlier_block(sn[SUB - 1, here, :]),
            ))
        return values

    def turn_cells(n):
        s = lax.div(n, passes)
        return [rows_beside(t, s, start((n - s * passes) * PAIR + k)) for k in range(PAIR)]

    def keep(values):
        for k, group in enumerate(values):
            for i, value in enumerate(group):
                beside[k, i] = value

    def prepare(b):
        turned = [[beside[k, i] for i in range(3)] for k in range(PAIR)]
        later = turn_coefficients(jnp.minimum(b + 1, passes - 1))
        for k in range(PAIR):
            at = start(b * PAIR + k)
            for j in range(SUB):
                t[0, j, pl.ds(at, SUB), :] = t0[j, pl.ds(at, SUB), :]
            all_coefficients(se, sn, kw, face, low, at, *turned[k])
        keep(later)

    keep(turn_coefficients(0))
    loop(passes, prepare)
    keep(turn_cells(0))

    def step(n):
        turned = [[beside[k, i] for i in range(4)] for k in range(PAIR)]
        s = lax.div(n, passes)
        later = turn_cells(jnp.minimum(n + 1, STEPS * passes - 1))
        for k in range(PAIR):
            advance(t, face, low, s, start((n - s * passes) * PAIR + k), turned[k], fluxes)
        keep(later)

    loop(STEPS * passes, step)


def frame_kernel(t_in, face_in, se_in, sn_in, kw_in, low_in, r0, r1, out, t, face, se, sn, kw, low, tall, done):
    cols = t.shape[3]
    planes, rows = out.shape[:2]
    height = tall.shape[0] // planes
    lon_even, _, top = parities()
    shape = (SUB, cols)
    lane = lanes(shape)
    sub = lax.broadcasted_iota(jnp.int32, shape, 0)
    left = lane < cols // 2
    fold = top & ((lane & (height // SUB - 1)) == height // SUB - 1)
    end = SUB + cols

    def halves(value):
        other = pltpu.roll(value, cols // 2, 1)
        return jnp.where(left, value, other), jnp.where(left, other, value)

    def unpack(j):
        for west in (False, True):
            def piece(i):
                at = pl.ds((KINDS * j + i) * HALO + (0 if west else 2), SUB)
                a, b = r0[at, :], r1[at, :]
                return jnp.where(lon_even, b, a) if west else jnp.where(lon_even, a, b)

            here = pl.ds(0 if west else end, SUB)
            t[0, j, here, :] = piece(0)
            speed, northern = halves(piece(1))
            kappa, wet = halves(piece(2))
            sn[j, here, :] = northern
            kw[j, here, :] = jnp.where(wet > 0, kappa, -1.0)
            if west:
                kept = (sub == SUB - 1) & fold
            else:
                here = pl.ds(end - 1, SUB)
                kept = (sub == 0) & jnp.logical_not(fold)
            se[j, here, :] = jnp.where(kept, se[j, here, :], speed)

    def unpack_two(i):
        for k in range(2):
            unpack(2 * i + k)

    loop(SUB // 2, unpack_two)
    for at in (0, end - 1):
        here = pl.ds(at, SUB)
        all_coefficients(
            se, sn, kw, face, low, at,
            earlier_block(kw[SUB - 1, here, :]), later_block(kw[0, here, :]), earlier_block(sn[SUB - 1, here, :]),
        )

    def step(s):
        west = SUB - 2 * (STEPS - 1) + 2 * s
        east = end - SUB + 2 * (STEPS - 1) - 2 * s
        beside = [rows_beside(t, s, at) for at in (west, east)]
        for at, rows_turned in zip((west, east), beside):
            advance(t, face, low, s, at, rows_turned)

    loop(STEPS, step)

    def transpose(i):
        n = height // SUB
        for k in range(4):
            j = 4 * i + k
            matrix = t[STEPS, j, pl.ds(SUB, cols), :].T
            for p in range(planes):
                tall[pl.ds(p * height + j, n, stride=SUB), :] = matrix[p * n : (p + 1) * n]

    loop(SUB // 4, transpose)
    copy = pltpu.make_async_copy(
        tall.reshape(planes, height, cols).at[:, pl.ds(SUB, rows), :], out, done
    )
    copy.start()
    copy.wait()


def call(kernel, shapes, *operands, specs=None, outs=None, grant=SMALL, scratch=(), alias=None):
    return pl.pallas_call(
        kernel,
        out_shape=[jax.ShapeDtypeStruct(s, jnp.float32) for s in shapes],
        in_specs=specs or [VMEM] * len(operands),
        out_specs=outs or [VMEM] * len(shapes),
        scratch_shapes=[pltpu.VMEM(s, jnp.float32) if isinstance(s, tuple) else s for s in scratch],
        input_output_aliases=alias or {},
        compiler_params=pltpu.CompilerParams(vmem_limit_bytes=grant),
        cost_estimate=pl.CostEstimate(flops=1 << 20, bytes_accessed=1 << 20, transcendentals=0),
    )(*operands)


def lon_swap(sizes, parity):
    lon, lat = sizes
    pairs = []
    for i in range(lon):
        other = (i + 1 if i % 2 == parity else i - 1) % lon
        pairs += [(i * lat + j, other * lat + j) for j in range(lat)]
    return pairs


def lat_swap(sizes, parity):
    lon, lat = sizes
    pairs = []
    for i in range(lon):
        for j in range(lat):
            if j % 2 != parity:
                if j > 0:
                    pairs.append((i * lat + j, i * lat + j - 1))
            elif j + 1 < lat:
                pairs.append((i * lat + j, i * lat + j + 1))
            else:
                pairs.append((i * lat + j, (lon - 1 - i) * lat + j))
    return pairs


def per_device(tracers, east_courant, north_courant, diffusivity, wet_levels):
    count, lev, rows, cols = tracers.shape
    planes, tall = count * lev, rows + 2 * SUB
    assert planes * (tall // SUB) == cols and rows % SUB == 0
    sizes = (lax.axis_size("lon"), lax.axis_size("lat"))
    message = (MESSAGE, lev, cols)
    stack = (PLANES * lev + 1, rows, cols)
    own, x, y = call(
        stage_kernel, [stack, message, message],
        *(
            pltpu.with_memory_space_constraint(v, pltpu.HBM)
            for v in (tracers.reshape(planes, rows, cols), east_courant, north_courant, diffusivity, wet_levels)
        ),
        specs=[ANY] * 5,
        scratch=[pltpu.VMEM((rows, cols), jnp.int32), pltpu.SemaphoreType.DMA((5,))],
    )
    y = lax.ppermute(y, AXES, lat_swap(sizes, 1))
    x = lax.ppermute(x, AXES, lat_swap(sizes, 0))
    wide = (SUB, cols + 2 * SUB, cols)
    packed = (-(-(SUB * KINDS * HALO + SUB) // SUB) * SUB, cols)
    t0, se, sn, kw, p0, p1 = call(
        turn_kernel, [wide] * 4 + [packed] * 2, own, x, y,
        scratch=[(n * tall, cols) for n in (planes, lev, lev, lev)],
    )
    r1 = lax.ppermute(p1, AXES, lon_swap(sizes, 1))
    r0 = lax.ppermute(p0, AXES, lon_swap(sizes, 0))
    t, face, low = call(
        interior_kernel, [(STEPS + 1,) + wide, (6,) + wide, (3,) + wide[1:]], t0, se, sn, kw,
        scratch=[wide, (PAIR, 4, SUB, cols)],
    )
    out, *_ = call(
        frame_kernel, [(planes, rows, cols), t.shape, face.shape, wide, wide, wide, low.shape],
        t, face, se, sn, kw, low, r0, r1,
        outs=[ANY] + [VMEM] * 6, alias={i: i + 1 for i in range(6)},
        scratch=[(planes * tall, cols), pltpu.SemaphoreType.DMA],
    )
    return out.reshape(tracers.shape)


def solution(mesh):
    placed = (
        P(None, None, "lat", "lon"),
        P(None, "lat", "lon"),
        P(None, "lat", "lon"),
        P(None, "lat", "lon"),
        P("lat", "lon"),
    )
    return jax.shard_map(
        per_device,
        mesh=mesh,
        in_specs=placed,
        out_specs=P(None, None, "lat", "lon"),
        check_vma=False,
    )
```

```python
import jax
import jax.numpy as jnp
from jax import lax
from jax.experimental import pallas as pl
from jax.experimental.pallas import tpu as pltpu
from jax.sharding import PartitionSpec as P


STEPS = 3
HALO = 2 * STEPS
AXES = ("lon", "lat")
SUB = 8
FEW = HALO - 1
AT_SPEED, AT_KAPPA = SUB * HALO, SUB * HALO + SUB * FEW
AT_COUNT = AT_KAPPA + SUB // 2 * FEW
SPARE = 2
PAIR = 4
COLUMNS = -(-(SPARE + AT_COUNT + SUB) // SUB) * SUB
SMALL = 16 << 20
VMEM = pl.BlockSpec(memory_space=pltpu.VMEM)
ANY = pl.BlockSpec(memory_space=pl.ANY)

AT_T, AT_E, AT_N, AT_K, AT_WET, MESSAGE = 0, 12, 16, 21, 26, 27
N_E, N_N, N_K = HALO - 2, HALO - 1, HALO - 1


def lanes(shape):
    return lax.broadcasted_iota(jnp.int32, shape, len(shape) - 1)


def take(value, index):
    return jnp.take_along_axis(value, index, axis=1)


def later_block(value):
    return pltpu.roll(value, value.shape[1] - 1, 1)


def earlier_block(value):
    return pltpu.roll(value, 1, 1)


def loop(count, body):
    def step(i, _):
        body(i)
        return 0

    lax.fori_loop(0, count, step, 0)


def parities():
    lon_even = lax.rem(lax.axis_index("lon"), 2) == 0
    lat = lax.axis_index("lat")
    return lon_even, lax.rem(lat, 2) == 0, lat == lax.axis_size("lat") - 1


def edge_kernel(tr, ec, nc, kd, wet, x, y, trs, ecs, ncs, kds, wets, done):
    rows, cols = wet.shape
    lev = ec.shape[0]
    _, lat_even, _ = parities()
    copies = []
    for side, start in enumerate((0, rows - SUB)):
        for source, target in ((tr, trs), (ec, ecs), (nc, ncs), (kd, kds)):
            n = source.shape[0]
            copies.append((source.at[:, pl.ds(start, SUB), :], target.at[pl.ds(side * n, n)]))
        copies.append((wet.at[pl.ds(start, SUB), :], wets.at[pl.ds(side * SUB, SUB), :]))
    copies = [pltpu.make_async_copy(a, b, done.at[i]) for i, (a, b) in enumerate(copies)]
    for copy in copies:
        copy.start()
    for copy in copies:
        copy.wait()
    flat = [ref.reshape(ref.shape[0] * SUB, cols) for ref in (trs, ecs, ncs, kds)]
    for out, upper in ((x, lat_even), (y, jnp.logical_not(lat_even))):
        side = jnp.where(upper, 1, 0)
        sub = [jnp.where(upper, SUB - 1 - m, m) for m in range(HALO)]

        def plane(i, p, m):
            start = side * (flat[i].shape[0] // 2) + p * lev * SUB + sub[m]
            return flat[i][pl.ds(start, lev, stride=SUB), :]

        for m in range(HALO):
            for p in range(2):
                out[AT_T + 2 * m + p] = plane(0, p, m)
        for at, i, count in ((AT_E, 1, N_E), (AT_N, 2, N_N), (AT_K, 3, N_K)):
            for m in range(count):
                out[at + m] = plane(i, 0, m)
        out[AT_WET] = jnp.zeros((lev, cols), jnp.float32)
        for m in range(N_K):
            out[AT_WET, pl.ds(m, 1), :] = wets[pl.ds(side * SUB + sub[m], 1), :].astype(jnp.float32)


def fill_kernel(tr, ec, nc, kd, wet, te, ee, ne, ke, ce, wets, done):
    rows, cols = wet.shape
    lev = ec.shape[0]
    copies = [(wet, wets)]
    for source, target in ((kd, ke), (tr, te), (ec, ee), (nc, ne)):
        copies.append((source, target.at[:, pl.ds(SUB, rows), :]))
    copies = [pltpu.make_async_copy(a, b, done.at[i]) for i, (a, b) in enumerate(copies)]
    for copy in copies:
        copy.start()
    zero = jnp.zeros((SUB, cols), jnp.float32)

    def clear(p):
        for start in (0, SUB + rows):
            for target in (ee, ne, ke):
                target[p, pl.ds(start, SUB), :] = zero
            te[p, pl.ds(start, SUB), :] = zero
            te[p + lev, pl.ds(start, SUB), :] = zero

    loop(lev, clear)
    for start in (0, SUB + rows):
        ce[pl.ds(start, SUB), :] = zero
    for copy in copies:
        copy.wait()
    ce[pl.ds(SUB, rows), :] = wets[...].astype(jnp.float32)

    def dry(p):
        for b in range(rows // SUB):
            at = pl.ds(SUB + b * SUB, SUB)
            wet_cells = wets[pl.ds(b * SUB, SUB), :] > p
            ke[p, at, :] = jnp.where(wet_cells, ke[p, at, :], -1.0)

    loop(lev, dry)


def turn_kernel(te_in, ee_in, ne_in, ke_in, ce_in, x, y, te, ee, ne, ke, ce, t0, se, sn, kw, p0, p1, cw):
    planes, tall, cols = te.shape
    lev = ee.shape[0]
    te, ee, ne, ke = (ref.reshape(ref.shape[0] * tall, cols) for ref in (te, ee, ne, ke))
    lon_even, lat_even, top = parities()
    bottom = lax.axis_index("lat") == 0
    shape = (lev, cols)
    lane = lanes(shape)
    level = lax.broadcasted_iota(jnp.int32, shape, 0).astype(jnp.float32)
    zero = jnp.zeros((SUB, cols), jnp.float32)
    turn = jnp.where(top, -1.0, 1.0)
    cells = jnp.where(top, cols - 1 - lane, lane)
    faces = jnp.where(top, jnp.where(lane == cols - 1, cols - 1, cols - 2 - lane), lane)
    for north in (False, True):
        def piece(at):
            a, b = x[at], y[at]
            if north:
                return jnp.where(lat_even, a, b)
            return jnp.where(bottom, 0.0, jnp.where(lat_even, b, a))

        def put(target, row, value, first=0):
            target[pl.ds(first * tall + row, lev, stride=tall), :] = value

        def turned(value, index):
            return take(value, index) if north else value

        at = [tall - SUB + m if north else SUB - 1 - m for m in range(HALO)]
        for m in range(HALO):
            for i in range(2):
                put(te, at[m], turned(piece(AT_T + 2 * m + i), cells), i * lev)
        wets = piece(AT_WET)
        for m in range(N_K):
            counts = jnp.broadcast_to(wets[m : m + 1], shape)
            kappa = jnp.where(level < counts, piece(AT_K + m), -1.0)
            put(ke, at[m], turned(kappa, cells))
        wets = turned(wets, cells)
        for m in range(N_K):
            ce[pl.ds(at[m], 1), :] = wets[m : m + 1]
        for m in range(N_E):
            value = turned(piece(AT_E + m), faces)
            put(ee, at[m], turn * value if north else value)
        if north:
            speeds = [turn * take(piece(AT_N + m), cells) for m in range(N_N)]
            last = ne[pl.ds(tall - SUB - 1, lev, stride=tall), :]
            put(ne, tall - SUB - 1, jnp.where(top, 0.5 * (last + speeds[0]), last))
            for m in range(N_E):
                put(ne, at[m], jnp.where(top, speeds[m + 1], speeds[m]))
        else:
            for m in range(N_N):
                put(ne, at[m], piece(AT_N + m))

    def transpose(i):
        for j in (2 * i, 2 * i + 1):
            for source, target, n in ((te, t0, planes), (ee, se, lev), (ne, sn, lev), (ke, kw, lev)):
                parts = [source[pl.ds(p * tall + j, tall // SUB, stride=SUB), :] for p in range(n)]
                matrix = jnp.concatenate(parts * (planes // n), 0)
                target[j, pl.ds(SUB, cols), :] = matrix.T

    loop(SUB // 2, transpose)
    for j in range(SUB):
        se[j, pl.ds(SUB - 1, 1), :] = se[j, pl.ds(SUB + cols - 1, 1), :]

    parts = [ce[pl.ds(j, tall // SUB, stride=SUB), :] for j in range(SUB)]
    cw[pl.ds(SUB, cols), :] = jnp.concatenate(parts * (cols // tall), 0).T

    left = lanes((SUB, cols)) < cols // 2
    for out, eastern in ((p0, lon_even), (p1, jnp.logical_not(lon_even))):
        out[0:SUB, :] = zero
        far = pl.ds(jnp.where(eastern, SUB + cols - HALO, SUB), SUB)
        here = pl.ds(jnp.where(eastern, SUB + cols - FEW, SUB), SUB)
        faced = pl.ds(jnp.where(eastern, SUB + cols - FEW, SUB - 1), SUB)
        for j in range(SUB):
            out[pl.ds(SPARE + j * HALO, SUB), :] = t0[j, far, :]
        for j in range(SUB):
            out[pl.ds(SPARE + AT_SPEED + j * FEW, SUB), :] = jnp.where(left, se[j, faced, :], sn[j, here, :])
        for j in range(SUB // 2):
            kappa = jnp.where(left, kw[j, here, :], kw[j + SUB // 2, here, :])
            out[pl.ds(SPARE + AT_KAPPA + j * FEW, SUB), :] = jnp.maximum(kappa, 0.0)
        out[pl.ds(SPARE + AT_COUNT, SUB), :] = cw[here, :]


def coefficients(speed, kappa, other_kappa):
    wet = jnp.minimum(kappa, other_kappa) > 0
    speed = jnp.where(wet, speed, 0.0)
    magnitude = jnp.abs(speed)
    spread = jnp.minimum(speed, 0.0) - jnp.where(wet, 0.5 * (kappa + other_kappa), 0.0)
    return speed, spread, 0.5 * magnitude * (1.0 - magnitude)


def all_coefficients(se, sn, kw, face, low, at, kappa_low, kappa_high, north_low):
    here = pl.ds(at, SUB)
    kappa = [kw[j, here, :] for j in range(SUB)] + [kappa_high]
    for c, value in enumerate(coefficients(north_low, kappa_low, kappa[0])):
        low[c, here, :] = value
    for j in range(SUB):
        eastern = coefficients(se[j, here, :], kappa[j], kw[j, pl.ds(at + 1, SUB), :])
        northern = coefficients(sn[j, here, :], kappa[j], kappa[j + 1])
        for c, value in enumerate(eastern + northern):
            face[c, j, here, :] = value


def flux(cell, before, here, after, face):
    speed, spread, slope = face
    upslope = jnp.where(speed > 0, before, after)
    limited = jnp.maximum(
        jnp.minimum(here, upslope), jnp.minimum(jnp.maximum(here, upslope), 0.0)
    )
    return speed * cell + spread * here + slope * limited


def east_flux(t, face, s, j, at):
    behind, cell, after, beyond = (t[s, j, pl.ds(at + i, SUB), :] for i in (-1, 0, 1, 2))
    coefs = tuple(face[c, j, pl.ds(at, SUB), :] for c in range(3))
    return flux(cell, cell - behind, after - cell, beyond - after, coefs)


def advance(t, face, low, s, at, beside, fluxes=None):
    here = pl.ds(at, SUB)
    cell = [t[s, j, here, :] for j in range(SUB)]
    if fluxes is None:
        divergence = [
            east_flux(t, face, s, j, at) - east_flux(t, face, s, j, at - 1) for j in range(SUB)
        ]
    else:
        east = [east_flux(t, face, s, j, at) for j in range(SUB)]
        for j in range(SUB):
            fluxes[j, here, :] = east[j]
        divergence = [east[j] - fluxes[j, pl.ds(at - 1, SUB), :] for j in range(SUB)]
    rows = [beside[0], beside[1], *cell, beside[2], beside[3]]
    slope = [b - a for a, b in zip(rows, rows[1:])]
    north = []
    for j in range(-1, SUB):
        coefs = tuple(low[c, here, :] if j < 0 else face[3 + c, j, here, :] for c in range(3))
        north.append(flux(rows[j + 2], slope[j + 1], slope[j + 2], slope[j + 3], coefs))
    for j in range(SUB):
        t[s + 1, j, here, :] = cell[j] - divergence[j] - (north[j + 1] - north[j])


def rows_beside(t, s, at):
    here = pl.ds(at, SUB)
    before = [earlier_block(t[s, j, here, :]) for j in (SUB - 2, SUB - 1)]
    return before + [later_block(t[s, j, here, :]) for j in (0, 1)]


def interior_kernel(t0, se, sn, kw, t, face, low, fluxes, beside):
    cols = t.shape[3]
    passes = cols // SUB // PAIR

    def start(g):
        return pl.multiple_of(SUB + g * SUB, SUB)

    def turn_coefficients(b):
        values = []
        for k in range(PAIR):
            here = pl.ds(start(b * PAIR + k), SUB)
            values.append((
                earlier_block(kw[SUB - 1, here, :]),
                later_block(kw[0, here, :]),
                earlier_block(sn[SUB - 1, here, :]),
            ))
        return values

    def turn_cells(n):
        s = lax.div(n, passes)
        return [rows_beside(t, s, start((n - s * passes) * PAIR + k)) for k in range(PAIR)]

    def keep(values):
        for k, group in enumerate(values):
            for i, value in enumerate(group):
                beside[k, i] = value

    def prepare(b):
        turned = [[beside[k, i] for i in range(3)] for k in range(PAIR)]
        later = turn_coefficients(jnp.minimum(b + 1, passes - 1))
        for k in range(PAIR):
            at = start(b * PAIR + k)
            for j in range(SUB):
                t[0, j, pl.ds(at, SUB), :] = t0[j, pl.ds(at, SUB), :]
            all_coefficients(se, sn, kw, face, low, at, *turned[k])
        keep(later)

    keep(turn_coefficients(0))
    loop(passes, prepare)
    keep(turn_cells(0))

    def step(n):
        turned = [[beside[k, i] for i in range(4)] for k in range(PAIR)]
        s = lax.div(n, passes)
        later = turn_cells(jnp.minimum(n + 1, STEPS * passes - 1))
        for k in range(PAIR):
            advance(t, face, low, s, start((n - s * passes) * PAIR + k), turned[k], fluxes)
        keep(later)

    loop(STEPS * passes, step)


def frame_kernel(t_in, face_in, se_in, sn_in, kw_in, low_in, r0, r1, out, t, face, se, sn, kw, low, tall, done):
    cols = t.shape[3]
    planes, rows = out.shape[:2]
    height = tall.shape[0] // planes
    lon_even, _, top = parities()
    shape = (SUB, cols)
    lane = lanes(shape)
    sub = lax.broadcasted_iota(jnp.int32, shape, 0)
    left = lane < cols // 2
    blocks = height // SUB
    block = lane & (blocks - 1)
    level = (lax.shift_right_logical(lane, blocks.bit_length() - 1)) & (planes // 2 - 1)
    level = level.astype(jnp.float32)
    fold = top & (block == blocks - 1)
    end = SUB + cols

    def halves(value):
        other = pltpu.roll(value, cols // 2, 1)
        return jnp.where(left, value, other), jnp.where(left, other, value)

    for west in (False, True):
        def piece(at, n):
            rows_at = pl.ds(SPARE + at - (SUB - n if west else 0), SUB)
            a, b = r0[rows_at, :], r1[rows_at, :]
            return jnp.where(lon_even, b, a) if west else jnp.where(lon_even, a, b)

        here = pl.ds(0 if west else end, SUB)
        faced = here if west else pl.ds(end - 1, SUB)
        kept = (sub == SUB - 1) & fold if west else (sub == 0) & jnp.logical_not(fold)
        counts = piece(AT_COUNT, FEW)
        for j in range(SUB):
            t[0, j, here, :] = piece(j * HALO, HALO)
            speed, northern = halves(piece(AT_SPEED + j * FEW, FEW))
            sn[j, here, :] = northern
            se[j, faced, :] = jnp.where(kept, se[j, faced, :], speed)
        for j in range(SUB // 2):
            for row, kappa in zip((j, j + SUB // 2), halves(piece(AT_KAPPA + j * FEW, FEW))):
                wet = level < take(counts, block + row * blocks)
                kw[row, here, :] = jnp.where(wet, kappa, -1.0)
    for at in (0, end - 1):
        here = pl.ds(at, SUB)
        all_coefficients(
            se, sn, kw, face, low, at,
            earlier_block(kw[SUB - 1, here, :]), later_block(kw[0, here, :]), earlier_block(sn[SUB - 1, here, :]),
        )

    def step(s):
        west = SUB - 2 * (STEPS - 1) + 2 * s
        east = end - SUB + 2 * (STEPS - 1) - 2 * s
        beside = [rows_beside(t, s, at) for at in (west, east)]
        for at, rows_turned in zip((west, east), beside):
            advance(t, face, low, s, at, rows_turned)

    loop(STEPS, step)

    def transpose(i):
        n = height // SUB
        for k in range(4):
            j = 4 * i + k
            matrix = t[STEPS, j, pl.ds(SUB, cols), :].T
            for p in range(planes):
                tall[pl.ds(p * height + j, n, stride=SUB), :] = matrix[p * n : (p + 1) * n]

    loop(SUB // 4, transpose)
    copy = pltpu.make_async_copy(
        tall.reshape(planes, height, cols).at[:, pl.ds(SUB, rows), :], out, done
    )
    copy.start()
    copy.wait()


def call(kernel, shapes, *operands, specs=None, outs=None, grant=SMALL, scratch=(), alias=None):
    return pl.pallas_call(
        kernel,
        out_shape=[jax.ShapeDtypeStruct(s, jnp.float32) for s in shapes],
        in_specs=specs or [VMEM] * len(operands),
        out_specs=outs or [VMEM] * len(shapes),
        scratch_shapes=[pltpu.VMEM(s, jnp.float32) if isinstance(s, tuple) else s for s in scratch],
        input_output_aliases=alias or {},
        compiler_params=pltpu.CompilerParams(vmem_limit_bytes=grant),
        cost_estimate=pl.CostEstimate(flops=1 << 20, bytes_accessed=1 << 20, transcendentals=0),
    )(*operands)


def lon_swap(sizes, parity):
    lon, lat = sizes
    pairs = []
    for i in range(lon):
        other = (i + 1 if i % 2 == parity else i - 1) % lon
        pairs += [(i * lat + j, other * lat + j) for j in range(lat)]
    return pairs


def lat_swap(sizes, parity):
    lon, lat = sizes
    pairs = []
    for i in range(lon):
        for j in range(lat):
            if j % 2 != parity:
                other = (i, j - 1) if j > 0 else (i ^ 1, j)
            else:
                other = (i, j + 1) if j + 1 < lat else (lon - 1 - i, j)
            pairs.append((i * lat + j, other[0] * lat + other[1]))
    return pairs


def per_device(tracers, east_courant, north_courant, diffusivity, wet_levels):
    count, lev, rows, cols = tracers.shape
    planes, tall = count * lev, rows + 2 * SUB
    blocks = tall // SUB
    assert planes * blocks == cols and rows % SUB == 0
    assert blocks & (blocks - 1) == 0 and lev & (lev - 1) == 0 and blocks == lev == SUB
    sizes = (lax.axis_size("lon"), lax.axis_size("lat"))
    message = (MESSAGE, lev, cols)
    given = [
        pltpu.with_memory_space_constraint(v, pltpu.HBM)
        for v in (tracers.reshape(planes, rows, cols), east_courant, north_courant, diffusivity, wet_levels)
    ]
    x, y = call(
        edge_kernel, [message] * 2, *given, specs=[ANY] * 5,
        scratch=[(2 * n, SUB, cols) for n in (planes, lev, lev, lev)]
        + [pltpu.VMEM((2 * SUB, cols), jnp.int32), pltpu.SemaphoreType.DMA((10,))],
    )
    y = lax.ppermute(y, AXES, lat_swap(sizes, 1))
    x = lax.ppermute(x, AXES, lat_swap(sizes, 0))
    extended = [(n, tall, cols) for n in (planes, lev, lev, lev)] + [(tall, cols)]
    filled = call(
        fill_kernel, extended, *given, specs=[ANY] * 5,
        scratch=[pltpu.VMEM((rows, cols), jnp.int32), pltpu.SemaphoreType.DMA((5,))],
    )
    wide = (SUB, cols + 2 * SUB, cols)
    packed = (COLUMNS, cols)
    *_, t0, se, sn, kw, p0, p1 = call(
        turn_kernel, extended + [wide] * 4 + [packed] * 2, *filled, x, y, alias={i: i for i in range(5)},
        scratch=[wide[1:]],
    )
    r1 = lax.ppermute(p1, AXES, lon_swap(sizes, 1))
    r0 = lax.ppermute(p0, AXES, lon_swap(sizes, 0))
    t, face, low = call(
        interior_kernel, [(STEPS + 1,) + wide, (6,) + wide, (3,) + wide[1:]], t0, se, sn, kw,
        scratch=[wide, (PAIR, 4, SUB, cols)],
    )
    out, *_ = call(
        frame_kernel, [(planes, rows, cols), t.shape, face.shape, wide, wide, wide, low.shape],
        t, face, se, sn, kw, low, r0, r1,
        outs=[ANY] + [VMEM] * 6, alias={i: i + 1 for i in range(6)},
        scratch=[(planes * tall, cols), pltpu.SemaphoreType.DMA],
    )
    return out.reshape(tracers.shape)


def solution(mesh):
    placed = (
        P(None, None, "lat", "lon"),
        P(None, "lat", "lon"),
        P(None, "lat", "lon"),
        P(None, "lat", "lon"),
        P("lat", "lon"),
    )
    return jax.shard_map(
        per_device,
        mesh=mesh,
        in_specs=placed,
        out_specs=P(None, None, "lat", "lon"),
        check_vma=False,
    )
```

```python
import jax
import jax.numpy as jnp
from jax import lax
from jax.experimental import pallas as pl
from jax.experimental.pallas import tpu as pltpu
from jax.sharding import PartitionSpec as P


STEPS = 3
HALO = 2 * STEPS
AXES = ("lon", "lat")
SUB = 8
FEW = HALO - 1
AT_SPEED, AT_KAPPA = SUB * HALO, SUB * HALO + SUB * FEW
AT_COUNT = AT_KAPPA + SUB // 2 * FEW
SPARE = 2
PAIR = 4
COLUMNS = -(-(SPARE + AT_COUNT + SUB) // SUB) * SUB
SMALL = 16 << 20
VMEM = pl.BlockSpec(memory_space=pltpu.VMEM)
ANY = pl.BlockSpec(memory_space=pl.ANY)

AT_T, AT_E, AT_N, AT_K, AT_WET, MESSAGE = 0, 12, 16, 21, 26, 27
N_E, N_N, N_K = HALO - 2, HALO - 1, HALO - 1


def lanes(shape):
    return lax.broadcasted_iota(jnp.int32, shape, len(shape) - 1)


def take(value, index):
    return jnp.take_along_axis(value, index, axis=1)


def later_block(value):
    return pltpu.roll(value, value.shape[1] - 1, 1)


def earlier_block(value):
    return pltpu.roll(value, 1, 1)


def loop(count, body):
    def step(i, _):
        body(i)
        return 0

    lax.fori_loop(0, count, step, 0)


def parities():
    lon_even = lax.rem(lax.axis_index("lon"), 2) == 0
    lat = lax.axis_index("lat")
    return lon_even, lax.rem(lat, 2) == 0, lat == lax.axis_size("lat") - 1


def edge_kernel(tr, ec, nc, kd, wet, x, y, trs, ecs, ncs, kds, wets, done):
    rows, cols = wet.shape
    lev = ec.shape[0]
    _, lat_even, _ = parities()
    copies = []
    for side, start in enumerate((0, rows - SUB)):
        for source, target in ((tr, trs), (ec, ecs), (nc, ncs), (kd, kds)):
            n = source.shape[0]
            copies.append((source.at[:, pl.ds(start, SUB), :], target.at[pl.ds(side * n, n)]))
        copies.append((wet.at[pl.ds(start, SUB), :], wets.at[pl.ds(side * SUB, SUB), :]))
    copies = [pltpu.make_async_copy(a, b, done.at[i]) for i, (a, b) in enumerate(copies)]
    for copy in copies:
        copy.start()
    for copy in copies:
        copy.wait()
    flat = [ref.reshape(ref.shape[0] * SUB, cols) for ref in (trs, ecs, ncs, kds)]
    for out, upper in ((x, lat_even), (y, jnp.logical_not(lat_even))):
        side = jnp.where(upper, 1, 0)
        sub = [jnp.where(upper, SUB - 1 - m, m) for m in range(HALO)]

        def plane(i, p, m):
            start = side * (flat[i].shape[0] // 2) + p * lev * SUB + sub[m]
            return flat[i][pl.ds(start, lev, stride=SUB), :]

        for m in range(HALO):
            for p in range(2):
                out[AT_T + 2 * m + p] = plane(0, p, m)
        for at, i, count in ((AT_E, 1, N_E), (AT_N, 2, N_N), (AT_K, 3, N_K)):
            for m in range(count):
                out[at + m] = plane(i, 0, m)
        out[AT_WET] = jnp.zeros((lev, cols), jnp.float32)
        for m in range(N_K):
            out[AT_WET, pl.ds(m, 1), :] = wets[pl.ds(side * SUB + sub[m], 1), :].astype(jnp.float32)


def fill_kernel(tr, ec, nc, kd, wet, te, ee, ne, ke, ce, wets, done):
    rows, cols = wet.shape
    lev = ec.shape[0]
    copies = [(wet, wets)]
    for source, target in ((kd, ke), (tr, te), (ec, ee), (nc, ne)):
        copies.append((source, target.at[:, pl.ds(SUB, rows), :]))
    copies = [pltpu.make_async_copy(a, b, done.at[i]) for i, (a, b) in enumerate(copies)]
    for copy in copies:
        copy.start()
    zero = jnp.zeros((SUB, cols), jnp.float32)

    def clear(p):
        for start in (0, SUB + rows):
            for target in (ee, ne, ke):
                target[p, pl.ds(start, SUB), :] = zero
            te[p, pl.ds(start, SUB), :] = zero
            te[p + lev, pl.ds(start, SUB), :] = zero

    loop(lev, clear)
    for start in (0, SUB + rows):
        ce[pl.ds(start, SUB), :] = zero
    for copy in copies:
        copy.wait()
    ce[pl.ds(SUB, rows), :] = wets[...].astype(jnp.float32)

    def dry(p):
        for b in range(rows // SUB):
            at = pl.ds(SUB + b * SUB, SUB)
            wet_cells = wets[pl.ds(b * SUB, SUB), :] > p
            ke[p, at, :] = jnp.where(wet_cells, ke[p, at, :], -1.0)

    loop(lev, dry)


def turn_kernel(te_in, ee_in, ne_in, ke_in, ce_in, x, y, te, ee, ne, ke, ce, t0, sp, kh, p0, p1, cw):
    planes, tall, cols = te.shape
    lev = ee.shape[0]
    te, ee, ne, ke = (ref.reshape(ref.shape[0] * tall, cols) for ref in (te, ee, ne, ke))
    lon_even, lat_even, top = parities()
    bottom = lax.axis_index("lat") == 0
    shape = (lev, cols)
    lane = lanes(shape)
    level = lax.broadcasted_iota(jnp.int32, shape, 0).astype(jnp.float32)
    zero = jnp.zeros((SUB, cols), jnp.float32)
    turn = jnp.where(top, -1.0, 1.0)
    cells = jnp.where(top, cols - 1 - lane, lane)
    faces = jnp.where(top, jnp.where(lane == cols - 1, cols - 1, cols - 2 - lane), lane)
    for north in (False, True):
        def piece(at):
            a, b = x[at], y[at]
            if north:
                return jnp.where(lat_even, a, b)
            return jnp.where(bottom, 0.0, jnp.where(lat_even, b, a))

        def put(target, row, value, first=0):
            target[pl.ds(first * tall + row, lev, stride=tall), :] = value

        def turned(value, index):
            return take(value, index) if north else value

        at = [tall - SUB + m if north else SUB - 1 - m for m in range(HALO)]
        for m in range(HALO):
            for i in range(2):
                put(te, at[m], turned(piece(AT_T + 2 * m + i), cells), i * lev)
        wets = piece(AT_WET)
        for m in range(N_K):
            counts = jnp.broadcast_to(wets[m : m + 1], shape)
            kappa = jnp.where(level < counts, piece(AT_K + m), -1.0)
            put(ke, at[m], turned(kappa, cells))
        wets = turned(wets, cells)
        for m in range(N_K):
            ce[pl.ds(at[m], 1), :] = wets[m : m + 1]
        for m in range(N_E):
            value = turned(piece(AT_E + m), faces)
            put(ee, at[m], turn * value if north else value)
        if north:
            speeds = [turn * take(piece(AT_N + m), cells) for m in range(N_N)]
            last = ne[pl.ds(tall - SUB - 1, lev, stride=tall), :]
            put(ne, tall - SUB - 1, jnp.where(top, 0.5 * (last + speeds[0]), last))
            for m in range(N_E):
                put(ne, at[m], jnp.where(top, speeds[m + 1], speeds[m]))
        else:
            for m in range(N_N):
                put(ne, at[m], piece(AT_N + m))

    def rows_of(source, j, n):
        return [source[pl.ds(p * tall + j, tall // SUB, stride=SUB), :] for p in range(n)]

    def transpose(i):
        for k in range(SUB // 4):
            j = i * (SUB // 4) + k
            for row in (2 * j, 2 * j + 1):
                t0[row, pl.ds(SUB, cols), :] = jnp.concatenate(rows_of(te, row, planes), 0).T
                both = rows_of(ee, row, lev) + rows_of(ne, row, lev)
                sp[row, pl.ds(SUB, cols), :] = jnp.concatenate(both, 0).T
            both = rows_of(ke, j, lev) + rows_of(ke, j + SUB // 2, lev)
            kh[j, pl.ds(SUB, cols), :] = jnp.concatenate(both, 0).T

    loop(2, transpose)
    for j in range(SUB):
        sp[j, pl.ds(SUB - 1, 1), :] = sp[j, pl.ds(SUB + cols - 1, 1), :]

    parts = [ce[pl.ds(j, tall // SUB, stride=SUB), :] for j in range(SUB)]
    cw[pl.ds(SUB, cols), :] = jnp.concatenate(parts * (cols // tall), 0).T

    left = lanes((SUB, cols)) < cols // 2
    for out, eastern in ((p0, lon_even), (p1, jnp.logical_not(lon_even))):
        out[0:SUB, :] = zero
        far = pl.ds(jnp.where(eastern, SUB + cols - HALO, SUB), SUB)
        here = pl.ds(jnp.where(eastern, SUB + cols - FEW, SUB), SUB)
        faced = pl.ds(jnp.where(eastern, SUB + cols - FEW, SUB - 1), SUB)
        for j in range(SUB):
            out[pl.ds(SPARE + j * HALO, SUB), :] = t0[j, far, :]
        for j in range(SUB):
            out[pl.ds(SPARE + AT_SPEED + j * FEW, SUB), :] = jnp.where(left, sp[j, faced, :], sp[j, here, :])
        for j in range(SUB // 2):
            out[pl.ds(SPARE + AT_KAPPA + j * FEW, SUB), :] = jnp.maximum(kh[j, here, :], 0.0)
        out[pl.ds(SPARE + AT_COUNT, SUB), :] = cw[here, :]


def coefficients(speed, kappa, other_kappa):
    wet = jnp.minimum(kappa, other_kappa) > 0
    speed = jnp.where(wet, speed, 0.0)
    magnitude = jnp.abs(speed)
    spread = jnp.minimum(speed, 0.0) - jnp.where(wet, 0.5 * (kappa + other_kappa), 0.0)
    return speed, spread, 0.5 * magnitude * (1.0 - magnitude)


def all_coefficients(se, sn, kw, face, low, at, kappa_low, kappa_high, north_low):
    here = pl.ds(at, SUB)
    kappa = [kw[j, here, :] for j in range(SUB)] + [kappa_high]
    for c, value in enumerate(coefficients(north_low, kappa_low, kappa[0])):
        low[c, here, :] = value
    for j in range(SUB):
        eastern = coefficients(se[j, here, :], kappa[j], kw[j, pl.ds(at + 1, SUB), :])
        northern = coefficients(sn[j, here, :], kappa[j], kappa[j + 1])
        for c, value in enumerate(eastern + northern):
            face[c, j, here, :] = value


def flux(cell, before, here, after, face):
    speed, spread, slope = face
    upslope = jnp.where(speed > 0, before, after)
    limited = jnp.maximum(
        jnp.minimum(here, upslope), jnp.minimum(jnp.maximum(here, upslope), 0.0)
    )
    return speed * cell + spread * here + slope * limited


def east_flux(t, face, s, j, at):
    behind, cell, after, beyond = (t[s, j, pl.ds(at + i, SUB), :] for i in (-1, 0, 1, 2))
    coefs = tuple(face[c, j, pl.ds(at, SUB), :] for c in range(3))
    return flux(cell, cell - behind, after - cell, beyond - after, coefs)


def advance(t, face, low, s, at, beside, fluxes=None):
    here = pl.ds(at, SUB)
    cell = [t[s, j, here, :] for j in range(SUB)]
    if fluxes is None:
        divergence = [
            east_flux(t, face, s, j, at) - east_flux(t, face, s, j, at - 1) for j in range(SUB)
        ]
    else:
        east = [east_flux(t, face, s, j, at) for j in range(SUB)]
        for j in range(SUB):
            fluxes[j, here, :] = east[j]
        divergence = [east[j] - fluxes[j, pl.ds(at - 1, SUB), :] for j in range(SUB)]
    rows = [beside[0], beside[1], *cell, beside[2], beside[3]]
    slope = [b - a for a, b in zip(rows, rows[1:])]
    north = []
    for j in range(-1, SUB):
        coefs = tuple(low[c, here, :] if j < 0 else face[3 + c, j, here, :] for c in range(3))
        north.append(flux(rows[j + 2], slope[j + 1], slope[j + 2], slope[j + 3], coefs))
    for j in range(SUB):
        t[s + 1, j, here, :] = cell[j] - divergence[j] - (north[j + 1] - north[j])


def rows_beside(t, s, at):
    here = pl.ds(at, SUB)
    before = [earlier_block(t[s, j, here, :]) for j in (SUB - 2, SUB - 1)]
    return before + [later_block(t[s, j, here, :]) for j in (0, 1)]


def interior_kernel(t0, sp, kh, t, face, low, se, sn, kw, fluxes, beside):
    cols = t.shape[3]
    passes = cols // SUB // PAIR

    def start(g):
        return pl.multiple_of(SUB + g * SUB, SUB)

    lane = lanes((SUB, cols))
    half = cols // 2
    left = lane < half
    within = lane & (half - 1)
    before = half + ((within - 1) & (half - 1))
    after = (within + 1) & (half - 1)

    def halves(value):
        other = pltpu.roll(value, half, 1)
        return jnp.where(left, value, other), jnp.where(left, other, value)

    def turn_coefficients(b):
        values = []
        for k in range(PAIR):
            here = pl.ds(start(b * PAIR + k), SUB)
            values.append((
                take(kh[SUB // 2 - 1, here, :], before), take(kh[0, here, :], after), take(sp[SUB - 1, here, :], before)
            ))
        return values

    def spread(b):
        values = []
        for k in range(PAIR):
            here = pl.ds(start(b * PAIR + k), SUB)
            speeds = [halves(sp[j, here, :]) for j in range(SUB)]
            values.append((here, speeds, [halves(kh[j, here, :]) for j in range(SUB // 2)]))
        return values

    def put_spread(values):
        for here, speeds, kappas in values:
            for j, (eastern, northern) in enumerate(speeds):
                se[j, here, :], sn[j, here, :] = eastern, northern
            for j, (lower, upper) in enumerate(kappas):
                kw[j, here, :], kw[j + SUB // 2, here, :] = lower, upper

    def turn_cells(n):
        s = lax.div(n, passes)
        return [rows_beside(t, s, start((n - s * passes) * PAIR + k)) for k in range(PAIR)]

    def keep(values):
        for k, group in enumerate(values):
            for i, value in enumerate(group):
                beside[k, i] = value

    def prepare(n):
        b = jnp.maximum(n - 1, 0)
        turned = [[beside[k, i] for i in range(3)] for k in range(PAIR)]
        following = jnp.minimum(n, passes - 1)
        later = turn_coefficients(following)
        values = spread(following)
        for k in range(PAIR):
            if k == PAIR - 1:
                put_spread(values)
            at = start(b * PAIR + k)
            for j in range(SUB):
                t[0, j, pl.ds(at, SUB), :] = t0[j, pl.ds(at, SUB), :]
            all_coefficients(se, sn, kw, face, low, at, *turned[k])
        keep(later)

    wrapped = [halves(sp[j, 0:SUB, :])[0] for j in range(SUB)]
    loop(passes + 1, prepare)
    for j in range(SUB):
        se[j, 0:SUB, :] = wrapped[j]
    keep(turn_cells(0))

    def step(n):
        turned = [[beside[k, i] for i in range(4)] for k in range(PAIR)]
        s = lax.div(n, passes)
        later = turn_cells(jnp.minimum(n + 1, STEPS * passes - 1))
        for k in range(PAIR):
            advance(t, face, low, s, start((n - s * passes) * PAIR + k), turned[k], fluxes)
        keep(later)

    loop(STEPS * passes, step)


def frame_kernel(t_in, face_in, se_in, sn_in, kw_in, low_in, r0, r1, out, t, face, se, sn, kw, low, tall, done):
    cols = t.shape[3]
    planes, rows = out.shape[:2]
    height = tall.shape[0] // planes
    lon_even, _, top = parities()
    shape = (SUB, cols)
    lane = lanes(shape)
    sub = lax.broadcasted_iota(jnp.int32, shape, 0)
    left = lane < cols // 2
    blocks = height // SUB
    block = lane & (blocks - 1)
    level = (lax.shift_right_logical(lane, blocks.bit_length() - 1)) & (planes // 2 - 1)
    level = level.astype(jnp.float32)
    fold = top & (block == blocks - 1)
    end = SUB + cols

    def halves(value):
        other = pltpu.roll(value, cols // 2, 1)
        return jnp.where(left, value, other), jnp.where(left, other, value)

    for west in (False, True):
        def piece(at, n):
            rows_at = pl.ds(SPARE + at - (SUB - n if west else 0), SUB)
            a, b = r0[rows_at, :], r1[rows_at, :]
            return jnp.where(lon_even, b, a) if west else jnp.where(lon_even, a, b)

        here = pl.ds(0 if west else end, SUB)
        faced = here if west else pl.ds(end - 1, SUB)
        kept = (sub == SUB - 1) & fold if west else (sub == 0) & jnp.logical_not(fold)
        counts = piece(AT_COUNT, FEW)
        for j in range(SUB):
            t[0, j, here, :] = piece(j * HALO, HALO)
            speed, northern = halves(piece(AT_SPEED + j * FEW, FEW))
            sn[j, here, :] = northern
            se[j, faced, :] = jnp.where(kept, se[j, faced, :], speed)
        for j in range(SUB // 2):
            for row, kappa in zip((j, j + SUB // 2), halves(piece(AT_KAPPA + j * FEW, FEW))):
                wet = level < take(counts, block + row * blocks)
                kw[row, here, :] = jnp.where(wet, kappa, -1.0)
    for at in (0, end - 1):
        here = pl.ds(at, SUB)
        all_coefficients(
            se, sn, kw, face, low, at,
            earlier_block(kw[SUB - 1, here, :]), later_block(kw[0, here, :]), earlier_block(sn[SUB - 1, here, :]),
        )

    def step(s):
        west = SUB - 2 * (STEPS - 1) + 2 * s
        east = end - SUB + 2 * (STEPS - 1) - 2 * s
        beside = [rows_beside(t, s, at) for at in (west, east)]
        for at, rows_turned in zip((west, east), beside):
            advance(t, face, low, s, at, rows_turned)

    loop(STEPS, step)

    def transpose(i):
        n = height // SUB
        for k in range(4):
            j = 4 * i + k
            matrix = t[STEPS, j, pl.ds(SUB, cols), :].T
            for p in range(planes):
                tall[pl.ds(p * height + j, n, stride=SUB), :] = matrix[p * n : (p + 1) * n]

    loop(SUB // 4, transpose)
    copy = pltpu.make_async_copy(
        tall.reshape(planes, height, cols).at[:, pl.ds(SUB, rows), :], out, done
    )
    copy.start()
    copy.wait()


def call(kernel, shapes, *operands, specs=None, outs=None, grant=SMALL, scratch=(), alias=None):
    return pl.pallas_call(
        kernel,
        out_shape=[jax.ShapeDtypeStruct(s, jnp.float32) for s in shapes],
        in_specs=specs or [VMEM] * len(operands),
        out_specs=outs or [VMEM] * len(shapes),
        scratch_shapes=[pltpu.VMEM(s, jnp.float32) if isinstance(s, tuple) else s for s in scratch],
        input_output_aliases=alias or {},
        compiler_params=pltpu.CompilerParams(vmem_limit_bytes=grant),
        cost_estimate=pl.CostEstimate(flops=1 << 20, bytes_accessed=1 << 20, transcendentals=0),
    )(*operands)


def lon_swap(sizes, parity):
    lon, lat = sizes
    pairs = []
    for i in range(lon):
        other = (i + 1 if i % 2 == parity else i - 1) % lon
        pairs += [(i * lat + j, other * lat + j) for j in range(lat)]
    return pairs


def lat_swap(sizes, parity):
    lon, lat = sizes
    pairs = []
    for i in range(lon):
        for j in range(lat):
            if j % 2 != parity:
                other = (i, j - 1) if j > 0 else (i ^ 1, j)
            else:
                other = (i, j + 1) if j + 1 < lat else (lon - 1 - i, j)
            pairs.append((i * lat + j, other[0] * lat + other[1]))
    return pairs


def per_device(tracers, east_courant, north_courant, diffusivity, wet_levels):
    count, lev, rows, cols = tracers.shape
    planes, tall = count * lev, rows + 2 * SUB
    blocks = tall // SUB
    assert planes * blocks == cols and rows % SUB == 0
    assert blocks & (blocks - 1) == 0 and lev & (lev - 1) == 0 and blocks == lev == SUB
    sizes = (lax.axis_size("lon"), lax.axis_size("lat"))
    message = (MESSAGE, lev, cols)
    given = [
        pltpu.with_memory_space_constraint(v, pltpu.HBM)
        for v in (tracers.reshape(planes, rows, cols), east_courant, north_courant, diffusivity, wet_levels)
    ]
    x, y = call(
        edge_kernel, [message] * 2, *given, specs=[ANY] * 5,
        scratch=[(2 * n, SUB, cols) for n in (planes, lev, lev, lev)]
        + [pltpu.VMEM((2 * SUB, cols), jnp.int32), pltpu.SemaphoreType.DMA((10,))],
    )
    y = lax.ppermute(y, AXES, lat_swap(sizes, 1))
    x = lax.ppermute(x, AXES, lat_swap(sizes, 0))
    extended = [(n, tall, cols) for n in (planes, lev, lev, lev)] + [(tall, cols)]
    filled = call(
        fill_kernel, extended, *given, specs=[ANY] * 5,
        scratch=[pltpu.VMEM((rows, cols), jnp.int32), pltpu.SemaphoreType.DMA((5,))],
    )
    wide = (SUB, cols + 2 * SUB, cols)
    packed = (COLUMNS, cols)
    *_, t0, sp, kh, p0, p1 = call(
        turn_kernel, extended + [wide] * 2 + [(SUB // 2,) + wide[1:]] + [packed] * 2, *filled, x, y, alias={i: i for i in range(5)},
        scratch=[wide[1:]],
    )
    r1 = lax.ppermute(p1, AXES, lon_swap(sizes, 1))
    r0 = lax.ppermute(p0, AXES, lon_swap(sizes, 0))
    t, face, low, se, sn, kw = call(
        interior_kernel, [(STEPS + 1,) + wide, (6,) + wide, (3,) + wide[1:]] + [wide] * 3, t0, sp, kh,
        scratch=[wide, (PAIR, 4, SUB, cols)],
    )
    out, *_ = call(
        frame_kernel, [(planes, rows, cols), t.shape, face.shape, wide, wide, wide, low.shape],
        t, face, se, sn, kw, low, r0, r1,
        outs=[ANY] + [VMEM] * 6, alias={i: i + 1 for i in range(6)},
        scratch=[(planes * tall, cols), pltpu.SemaphoreType.DMA],
    )
    return out.reshape(tracers.shape)


def solution(mesh):
    placed = (
        P(None, None, "lat", "lon"),
        P(None, "lat", "lon"),
        P(None, "lat", "lon"),
        P(None, "lat", "lon"),
        P("lat", "lon"),
    )
    return jax.shard_map(
        per_device,
        mesh=mesh,
        in_specs=placed,
        out_specs=P(None, None, "lat", "lon"),
        check_vma=False,
    )
```

```python
import jax
import jax.numpy as jnp
from jax import lax
from jax.experimental import pallas as pl
from jax.experimental.pallas import tpu as pltpu
from jax.sharding import PartitionSpec as P


STEPS = 3
HALO = 2 * STEPS
AXES = ("lon", "lat")
SUB = 8
FEW = HALO - 1
AT_SPEED, AT_KAPPA = SUB * HALO, SUB * HALO + SUB * FEW
AT_COUNT = AT_KAPPA + SUB // 2 * FEW
SPARE = 2
PAIR = 4
COLUMNS = -(-(SPARE + AT_COUNT + SUB) // SUB) * SUB
SMALL = 16 << 20
VMEM = pl.BlockSpec(memory_space=pltpu.VMEM)
ANY = pl.BlockSpec(memory_space=pl.ANY)

AT_T, AT_E, AT_N, AT_K, AT_WET, MESSAGE = 0, 12, 16, 21, 26, 27
N_E, N_N, N_K = HALO - 2, HALO - 1, HALO - 1


def lanes(shape):
    return lax.broadcasted_iota(jnp.int32, shape, len(shape) - 1)


def take(value, index):
    return jnp.take_along_axis(value, index, axis=1)


def later_block(value):
    return pltpu.roll(value, value.shape[1] - 1, 1)


def earlier_block(value):
    return pltpu.roll(value, 1, 1)


def loop(count, body):
    def step(i, _):
        body(i)
        return 0

    lax.fori_loop(0, count, step, 0)


def parities():
    lon_even = lax.rem(lax.axis_index("lon"), 2) == 0
    lat = lax.axis_index("lat")
    return lon_even, lax.rem(lat, 2) == 0, lat == lax.axis_size("lat") - 1


def edge_kernel(tr, ec, nc, kd, wet, x, y, trs, ecs, ncs, kds, wets, done):
    rows, cols = wet.shape
    lev = ec.shape[0]
    _, lat_even, _ = parities()
    copies = []
    for side, start in enumerate((0, rows - SUB)):
        for source, target in ((tr, trs), (ec, ecs), (nc, ncs), (kd, kds)):
            n = source.shape[0]
            copies.append((source.at[:, pl.ds(start, SUB), :], target.at[pl.ds(side * n, n)]))
        copies.append((wet.at[pl.ds(start, SUB), :], wets.at[pl.ds(side * SUB, SUB), :]))
    copies = [pltpu.make_async_copy(a, b, done.at[i]) for i, (a, b) in enumerate(copies)]
    for copy in copies:
        copy.start()
    for copy in copies:
        copy.wait()
    flat = [ref.reshape(ref.shape[0] * SUB, cols) for ref in (trs, ecs, ncs, kds)]
    for out, upper in ((x, lat_even), (y, jnp.logical_not(lat_even))):
        side = jnp.where(upper, 1, 0)
        sub = [jnp.where(upper, SUB - 1 - m, m) for m in range(HALO)]

        def plane(i, p, m):
            start = side * (flat[i].shape[0] // 2) + p * lev * SUB + sub[m]
            return flat[i][pl.ds(start, lev, stride=SUB), :]

        for m in range(HALO):
            for p in range(2):
                out[AT_T + 2 * m + p] = plane(0, p, m)
        for at, i, count in ((AT_E, 1, N_E), (AT_N, 2, N_N), (AT_K, 3, N_K)):
            for m in range(count):
                out[at + m] = plane(i, 0, m)
        out[AT_WET] = jnp.zeros((lev, cols), jnp.float32)
        for m in range(N_K):
            out[AT_WET, pl.ds(m, 1), :] = wets[pl.ds(side * SUB + sub[m], 1), :].astype(jnp.float32)


def fill_kernel(tr, ec, nc, kd, wet, te, ee, ne, ke, ce, wets, done):
    rows, cols = wet.shape
    lev = ec.shape[0]
    copies = [(wet, wets)]
    for source, target in ((kd, ke), (tr, te), (ec, ee), (nc, ne)):
        copies.append((source, target.at[:, pl.ds(SUB, rows), :]))
    copies = [pltpu.make_async_copy(a, b, done.at[i]) for i, (a, b) in enumerate(copies)]
    for copy in copies:
        copy.start()
    zero = jnp.zeros((SUB, cols), jnp.float32)

    def clear(p):
        for start in (0, SUB + rows):
            for target in (ee, ne, ke):
                target[p, pl.ds(start, SUB), :] = zero
            te[p, pl.ds(start, SUB), :] = zero
            te[p + lev, pl.ds(start, SUB), :] = zero

    loop(lev, clear)
    for start in (0, SUB + rows):
        ce[pl.ds(start, SUB), :] = zero
    for copy in copies:
        copy.wait()
    ce[pl.ds(SUB, rows), :] = wets[...].astype(jnp.float32)

    def dry(p):
        for b in range(rows // SUB):
            at = pl.ds(SUB + b * SUB, SUB)
            wet_cells = wets[pl.ds(b * SUB, SUB), :] > p
            ke[p, at, :] = jnp.where(wet_cells, ke[p, at, :], -1.0)

    loop(lev, dry)


def turn_kernel(te_in, ee_in, ne_in, ke_in, ce_in, x, y, te, ee, ne, ke, ce, t0, sp, kh, p0, p1, cw):
    planes, tall, cols = te.shape
    lev = ee.shape[0]
    te, ee, ne, ke = (ref.reshape(ref.shape[0] * tall, cols) for ref in (te, ee, ne, ke))
    lon_even, lat_even, top = parities()
    bottom = lax.axis_index("lat") == 0
    shape = (lev, cols)
    lane = lanes(shape)
    level = lax.broadcasted_iota(jnp.int32, shape, 0).astype(jnp.float32)
    zero = jnp.zeros((SUB, cols), jnp.float32)
    turn = jnp.where(top, -1.0, 1.0)
    cells = jnp.where(top, cols - 1 - lane, lane)
    faces = jnp.where(top, jnp.where(lane == cols - 1, cols - 1, cols - 2 - lane), lane)
    for north in (False, True):
        def piece(at):
            a, b = x[at], y[at]
            if north:
                return jnp.where(lat_even, a, b)
            return jnp.where(bottom, 0.0, jnp.where(lat_even, b, a))

        def put(target, row, value, first=0):
            target[pl.ds(first * tall + row, lev, stride=tall), :] = value

        def turned(value, index):
            return take(value, index) if north else value

        at = [tall - SUB + m if north else SUB - 1 - m for m in range(HALO)]
        for m in range(HALO):
            for i in range(2):
                put(te, at[m], turned(piece(AT_T + 2 * m + i), cells), i * lev)
        wets = piece(AT_WET)
        for m in range(N_K):
            counts = jnp.broadcast_to(wets[m : m + 1], shape)
            kappa = jnp.where(level < counts, piece(AT_K + m), -1.0)
            put(ke, at[m], turned(kappa, cells))
        wets = turned(wets, cells)
        for m in range(N_K):
            ce[pl.ds(at[m], 1), :] = wets[m : m + 1]
        for m in range(N_E):
            value = turned(piece(AT_E + m), faces)
            put(ee, at[m], turn * value if north else value)
        if north:
            speeds = [turn * take(piece(AT_N + m), cells) for m in range(N_N)]
            last = ne[pl.ds(tall - SUB - 1, lev, stride=tall), :]
            put(ne, tall - SUB - 1, jnp.where(top, 0.5 * (last + speeds[0]), last))
            for m in range(N_E):
                put(ne, at[m], jnp.where(top, speeds[m + 1], speeds[m]))
        else:
            for m in range(N_N):
                put(ne, at[m], piece(AT_N + m))

    def rows_of(source, j, n):
        return [source[pl.ds(p * tall + j, tall // SUB, stride=SUB), :] for p in range(n)]

    def transpose(i):
        for k in range(SUB // 4):
            j = i * (SUB // 4) + k
            for row in (2 * j, 2 * j + 1):
                t0[row, pl.ds(SUB, cols), :] = jnp.concatenate(rows_of(te, row, planes), 0).T
                both = rows_of(ee, row, lev) + rows_of(ne, row, lev)
                sp[row, pl.ds(SUB, cols), :] = jnp.concatenate(both, 0).T
            both = rows_of(ke, j, lev) + rows_of(ke, j + SUB // 2, lev)
            kh[j, pl.ds(SUB, cols), :] = jnp.concatenate(both, 0).T

    loop(2, transpose)
    for j in range(SUB):
        sp[j, pl.ds(SUB - 1, 1), :] = sp[j, pl.ds(SUB + cols - 1, 1), :]

    parts = [ce[pl.ds(j, tall // SUB, stride=SUB), :] for j in range(SUB)]
    cw[pl.ds(SUB, cols), :] = jnp.concatenate(parts * (cols // tall), 0).T

    left = lanes((SUB, cols)) < cols // 2
    for out, eastern in ((p0, lon_even), (p1, jnp.logical_not(lon_even))):
        out[0:SUB, :] = zero
        far = pl.ds(jnp.where(eastern, SUB + cols - HALO, SUB), SUB)
        here = pl.ds(jnp.where(eastern, SUB + cols - FEW, SUB), SUB)
        faced = pl.ds(jnp.where(eastern, SUB + cols - FEW, SUB - 1), SUB)
        for j in range(SUB):
            out[pl.ds(SPARE + j * HALO, SUB), :] = t0[j, far, :]
        for j in range(SUB):
            out[pl.ds(SPARE + AT_SPEED + j * FEW, SUB), :] = jnp.where(left, sp[j, faced, :], sp[j, here, :])
        for j in range(SUB // 2):
            out[pl.ds(SPARE + AT_KAPPA + j * FEW, SUB), :] = jnp.maximum(kh[j, here, :], 0.0)
        out[pl.ds(SPARE + AT_COUNT, SUB), :] = cw[here, :]


def coefficients(speed, kappa, other_kappa):
    wet = jnp.minimum(kappa, other_kappa) > 0
    speed = jnp.where(wet, speed, 0.0)
    magnitude = jnp.abs(speed)
    spread = jnp.minimum(speed, 0.0) - jnp.where(wet, 0.5 * (kappa + other_kappa), 0.0)
    return speed, spread, 0.5 * magnitude * (1.0 - magnitude)


def all_coefficients(se, sn, kw, face, low, at, kappa_low, kappa_high, north_low):
    here = pl.ds(at, SUB)
    kappa = [kw[j, here, :] for j in range(SUB)] + [kappa_high]
    for c, value in enumerate(coefficients(north_low, kappa_low, kappa[0])):
        low[c, here, :] = value
    for j in range(SUB):
        eastern = coefficients(se[j, here, :], kappa[j], kw[j, pl.ds(at + 1, SUB), :])
        northern = coefficients(sn[j, here, :], kappa[j], kappa[j + 1])
        for c, value in enumerate(eastern + northern):
            face[c, j, here, :] = value


def flux(cell, before, here, after, face):
    speed, spread, slope = face
    upslope = jnp.where(speed > 0, before, after)
    limited = jnp.maximum(
        jnp.minimum(here, upslope), jnp.minimum(jnp.maximum(here, upslope), 0.0)
    )
    return speed * cell + spread * here + slope * limited


def east_flux(t, face, s, j, at):
    behind, cell, after, beyond = (t[s, j, pl.ds(at + i, SUB), :] for i in (-1, 0, 1, 2))
    coefs = tuple(face[c, j, pl.ds(at, SUB), :] for c in range(3))
    return flux(cell, cell - behind, after - cell, beyond - after, coefs)


def advance(t, face, low, s, at, beside, fluxes=None):
    here = pl.ds(at, SUB)
    cell = [t[s, j, here, :] for j in range(SUB)]
    if fluxes is None:
        divergence = [
            east_flux(t, face, s, j, at) - east_flux(t, face, s, j, at - 1) for j in range(SUB)
        ]
    else:
        east = [east_flux(t, face, s, j, at) for j in range(SUB)]
        for j in range(SUB):
            fluxes[j, here, :] = east[j]
        divergence = [east[j] - fluxes[j, pl.ds(at - 1, SUB), :] for j in range(SUB)]
    rows = [beside[0], beside[1], *cell, beside[2], beside[3]]
    slope = [b - a for a, b in zip(rows, rows[1:])]
    north = []
    for j in range(-1, SUB):
        coefs = tuple(low[c, here, :] if j < 0 else face[3 + c, j, here, :] for c in range(3))
        north.append(flux(rows[j + 2], slope[j + 1], slope[j + 2], slope[j + 3], coefs))
    for j in range(SUB):
        t[s + 1, j, here, :] = cell[j] - divergence[j] - (north[j + 1] - north[j])


def rows_beside(t, s, at):
    here = pl.ds(at, SUB)
    before = [earlier_block(t[s, j, here, :]) for j in (SUB - 2, SUB - 1)]
    return before + [later_block(t[s, j, here, :]) for j in (0, 1)]


def interior_kernel(t0, sp, kh, t, face, low, se, sn, kw, fluxes, beside):
    cols = t.shape[3]
    passes = cols // SUB // PAIR

    def start(g):
        return pl.multiple_of(SUB + g * SUB, SUB)

    lane = lanes((SUB, cols))
    half = cols // 2
    left = lane < half
    within = lane & (half - 1)
    before = half + ((within - 1) & (half - 1))
    after = (within + 1) & (half - 1)

    def halves(value):
        other = pltpu.roll(value, half, 1)
        return jnp.where(left, value, other), jnp.where(left, other, value)

    def turn_coefficients(b):
        values = []
        for k in range(PAIR):
            here = pl.ds(start(b * PAIR + k), SUB)
            values.append((
                take(kh[SUB // 2 - 1, here, :], before), take(kh[0, here, :], after), take(sp[SUB - 1, here, :], before)
            ))
        return values

    def spread(b):
        values = []
        for k in range(PAIR):
            here = pl.ds(start(b * PAIR + k), SUB)
            speeds = [halves(sp[j, here, :]) for j in range(SUB)]
            values.append((here, speeds, [halves(kh[j, here, :]) for j in range(SUB // 2)]))
        return values

    def put_spread(values):
        for here, speeds, kappas in values:
            for j, (eastern, northern) in enumerate(speeds):
                se[j, here, :], sn[j, here, :] = eastern, northern
            for j, (lower, upper) in enumerate(kappas):
                kw[j, here, :], kw[j + SUB // 2, here, :] = lower, upper

    def turn_cells(n):
        s = lax.div(n, passes)
        return [rows_beside(t, s, start((n - s * passes) * PAIR + k)) for k in range(PAIR)]

    def keep(values):
        for k, group in enumerate(values):
            for i, value in enumerate(group):
                beside[k, i] = value

    def prepare(n):
        b = jnp.maximum(n - 1, 0)
        turned = [[beside[k, i] for i in range(3)] for k in range(PAIR)]
        following = jnp.minimum(n, passes - 1)
        later = turn_coefficients(following)
        values = spread(following)
        for k in range(PAIR):
            if k == PAIR - 1:
                put_spread(values)
            at = start(b * PAIR + k)
            for j in range(SUB):
                t[0, j, pl.ds(at, SUB), :] = t0[j, pl.ds(at, SUB), :]
            all_coefficients(se, sn, kw, face, low, at, *turned[k])
        keep(later)

    wrapped = [halves(sp[j, 0:SUB, :])[0] for j in range(SUB)]
    loop(passes + 1, prepare)
    for j in range(SUB):
        se[j, 0:SUB, :] = wrapped[j]
    keep(turn_cells(0))

    def step(n):
        turned = [[beside[k, i] for i in range(4)] for k in range(PAIR)]
        s = lax.div(n, passes)
        later = turn_cells(jnp.minimum(n + 1, STEPS * passes - 1))
        for k in range(PAIR):
            advance(t, face, low, s, start((n - s * passes) * PAIR + k), turned[k], fluxes)
        keep(later)

    loop(STEPS * passes, step)


def frame_kernel(t_in, face_in, se_in, sn_in, kw_in, low_in, r0, r1, out, t, face, se, sn, kw, low, tall, done):
    cols = t.shape[3]
    planes, rows = out.shape[:2]
    height = tall.shape[0] // planes
    lon_even, _, top = parities()
    shape = (SUB, cols)
    lane = lanes(shape)
    sub = lax.broadcasted_iota(jnp.int32, shape, 0)
    left = lane < cols // 2
    blocks = height // SUB
    block = lane & (blocks - 1)
    level = (lax.shift_right_logical(lane, blocks.bit_length() - 1)) & (planes // 2 - 1)
    level = level.astype(jnp.float32)
    fold = top & (block == blocks - 1)
    end = SUB + cols

    def halves(value):
        other = pltpu.roll(value, cols // 2, 1)
        return jnp.where(left, value, other), jnp.where(left, other, value)

    for west in (False, True):
        def piece(at, n):
            rows_at = pl.ds(SPARE + at - (SUB - n if west else 0), SUB)
            a, b = r0[rows_at, :], r1[rows_at, :]
            return jnp.where(lon_even, b, a) if west else jnp.where(lon_even, a, b)

        here = pl.ds(0 if west else end, SUB)
        faced = here if west else pl.ds(end - 1, SUB)
        kept = (sub == SUB - 1) & fold if west else (sub == 0) & jnp.logical_not(fold)
        counts = piece(AT_COUNT, FEW)
        for j in range(SUB):
            t[0, j, here, :] = piece(j * HALO, HALO)
            speed, northern = halves(piece(AT_SPEED + j * FEW, FEW))
            sn[j, here, :] = northern
            se[j, faced, :] = jnp.where(kept, se[j, faced, :], speed)
        for j in range(SUB // 2):
            for row, kappa in zip((j, j + SUB // 2), halves(piece(AT_KAPPA + j * FEW, FEW))):
                wet = level < take(counts, block + row * blocks)
                kw[row, here, :] = jnp.where(wet, kappa, -1.0)
    for at in (0, end - 1):
        here = pl.ds(at, SUB)
        all_coefficients(
            se, sn, kw, face, low, at,
            earlier_block(kw[SUB - 1, here, :]), later_block(kw[0, here, :]), earlier_block(sn[SUB - 1, here, :]),
        )

    def step(s):
        west = SUB - 2 * (STEPS - 1) + 2 * s
        east = end - SUB + 2 * (STEPS - 1) - 2 * s
        beside = [rows_beside(t, s, at) for at in (west, east)]
        for at, rows_turned in zip((west, east), beside):
            advance(t, face, low, s, at, rows_turned)

    for s in range(STEPS):
        step(s)

    def transpose(i):
        n = height // SUB
        for k in range(SUB):
            j = SUB * i + k
            matrix = t[STEPS, j, pl.ds(SUB, cols), :].T
            for p in range(planes):
                tall[pl.ds(p * height + j, n, stride=SUB), :] = matrix[p * n : (p + 1) * n]

    transpose(0)
    copy = pltpu.make_async_copy(
        tall.reshape(planes, height, cols).at[:, pl.ds(SUB, rows), :], out, done
    )
    copy.start()
    copy.wait()


def call(kernel, shapes, *operands, specs=None, outs=None, grant=SMALL, scratch=(), alias=None):
    return pl.pallas_call(
        kernel,
        out_shape=[jax.ShapeDtypeStruct(s, jnp.float32) for s in shapes],
        in_specs=specs or [VMEM] * len(operands),
        out_specs=outs or [VMEM] * len(shapes),
        scratch_shapes=[pltpu.VMEM(s, jnp.float32) if isinstance(s, tuple) else s for s in scratch],
        input_output_aliases=alias or {},
        compiler_params=pltpu.CompilerParams(vmem_limit_bytes=grant),
        cost_estimate=pl.CostEstimate(flops=1 << 20, bytes_accessed=1 << 20, transcendentals=0),
    )(*operands)


def lon_swap(sizes, parity):
    lon, lat = sizes
    pairs = []
    for i in range(lon):
        other = (i + 1 if i % 2 == parity else i - 1) % lon
        pairs += [(i * lat + j, other * lat + j) for j in range(lat)]
    return pairs


def lat_swap(sizes, parity):
    lon, lat = sizes
    pairs = []
    for i in range(lon):
        for j in range(lat):
            if j % 2 != parity:
                other = (i, j - 1) if j > 0 else (i ^ 1, j)
            else:
                other = (i, j + 1) if j + 1 < lat else (lon - 1 - i, j)
            pairs.append((i * lat + j, other[0] * lat + other[1]))
    return pairs


def per_device(tracers, east_courant, north_courant, diffusivity, wet_levels):
    count, lev, rows, cols = tracers.shape
    planes, tall = count * lev, rows + 2 * SUB
    blocks = tall // SUB
    assert planes * blocks == cols and rows % SUB == 0
    assert blocks & (blocks - 1) == 0 and lev & (lev - 1) == 0 and blocks == lev == SUB
    sizes = (lax.axis_size("lon"), lax.axis_size("lat"))
    message = (MESSAGE, lev, cols)
    given = [
        pltpu.with_memory_space_constraint(v, pltpu.HBM)
        for v in (tracers.reshape(planes, rows, cols), east_courant, north_courant, diffusivity, wet_levels)
    ]
    x, y = call(
        edge_kernel, [message] * 2, *given, specs=[ANY] * 5,
        scratch=[(2 * n, SUB, cols) for n in (planes, lev, lev, lev)]
        + [pltpu.VMEM((2 * SUB, cols), jnp.int32), pltpu.SemaphoreType.DMA((10,))],
    )
    y = lax.ppermute(y, AXES, lat_swap(sizes, 1))
    x = lax.ppermute(x, AXES, lat_swap(sizes, 0))
    extended = [(n, tall, cols) for n in (planes, lev, lev, lev)] + [(tall, cols)]
    filled = call(
        fill_kernel, extended, *given, specs=[ANY] * 5,
        scratch=[pltpu.VMEM((rows, cols), jnp.int32), pltpu.SemaphoreType.DMA((5,))],
    )
    wide = (SUB, cols + 2 * SUB, cols)
    packed = (COLUMNS, cols)
    *_, t0, sp, kh, p0, p1 = call(
        turn_kernel, extended + [wide] * 2 + [(SUB // 2,) + wide[1:]] + [packed] * 2, *filled, x, y, alias={i: i for i in range(5)},
        scratch=[wide[1:]],
    )
    r1 = lax.ppermute(p1, AXES, lon_swap(sizes, 1))
    r0 = lax.ppermute(p0, AXES, lon_swap(sizes, 0))
    t, face, low, se, sn, kw = call(
        interior_kernel, [(STEPS + 1,) + wide, (6,) + wide, (3,) + wide[1:]] + [wide] * 3, t0, sp, kh,
        scratch=[wide, (PAIR, 4, SUB, cols)],
    )
    out, *_ = call(
        frame_kernel, [(planes, rows, cols), t.shape, face.shape, wide, wide, wide, low.shape],
        t, face, se, sn, kw, low, r0, r1,
        outs=[ANY] + [VMEM] * 6, alias={i: i + 1 for i in range(6)},
        scratch=[(planes * tall, cols), pltpu.SemaphoreType.DMA],
    )
    return out.reshape(tracers.shape)


def solution(mesh):
    placed = (
        P(None, None, "lat", "lon"),
        P(None, "lat", "lon"),
        P(None, "lat", "lon"),
        P(None, "lat", "lon"),
        P("lat", "lon"),
    )
    return jax.shard_map(
        per_device,
        mesh=mesh,
        in_specs=placed,
        out_specs=P(None, None, "lat", "lon"),
        check_vma=False,
    )
```

```python
import jax
import jax.numpy as jnp
from jax import lax
from jax.experimental import pallas as pl
from jax.experimental.pallas import tpu as pltpu
from jax.sharding import PartitionSpec as P


STEPS = 3
HALO = 2 * STEPS
AXES = ("lon", "lat")
SUB = 8
FEW = HALO - 1
AT_SPEED, AT_KAPPA = SUB * HALO, SUB * HALO + SUB * FEW
AT_COUNT = AT_KAPPA + SUB // 2 * FEW
SPARE = 2
PAIR = 8
COLUMNS = -(-(SPARE + AT_COUNT + SUB) // SUB) * SUB
SMALL = 16 << 20
VMEM = pl.BlockSpec(memory_space=pltpu.VMEM)
ANY = pl.BlockSpec(memory_space=pl.ANY)

AT_T, AT_E, AT_N, AT_K, AT_WET, MESSAGE = 0, 12, 16, 21, 26, 27
N_E, N_N, N_K = HALO - 2, HALO - 1, HALO - 1


def lanes(shape):
    return lax.broadcasted_iota(jnp.int32, shape, len(shape) - 1)


def take(value, index):
    return jnp.take_along_axis(value, index, axis=1)


def later_block(value):
    return pltpu.roll(value, value.shape[1] - 1, 1)


def earlier_block(value):
    return pltpu.roll(value, 1, 1)


def loop(count, body):
    def step(i, _):
        body(i)
        return 0

    lax.fori_loop(0, count, step, 0)


def parities():
    lon_even = lax.rem(lax.axis_index("lon"), 2) == 0
    lat = lax.axis_index("lat")
    return lon_even, lax.rem(lat, 2) == 0, lat == lax.axis_size("lat") - 1


def edge_kernel(tr, ec, nc, kd, wet, x, y, trs, ecs, ncs, kds, wets, done):
    rows, cols = wet.shape
    lev = ec.shape[0]
    _, lat_even, _ = parities()
    copies = []
    for side, start in enumerate((0, rows - SUB)):
        for source, target in ((tr, trs), (ec, ecs), (nc, ncs), (kd, kds)):
            n = source.shape[0]
            copies.append((source.at[:, pl.ds(start, SUB), :], target.at[pl.ds(side * n, n)]))
        copies.append((wet.at[pl.ds(start, SUB), :], wets.at[pl.ds(side * SUB, SUB), :]))
    copies = [pltpu.make_async_copy(a, b, done.at[i]) for i, (a, b) in enumerate(copies)]
    for copy in copies:
        copy.start()
    for copy in copies:
        copy.wait()
    flat = [ref.reshape(ref.shape[0] * SUB, cols) for ref in (trs, ecs, ncs, kds)]
    for out, upper in ((x, lat_even), (y, jnp.logical_not(lat_even))):
        side = jnp.where(upper, 1, 0)
        sub = [jnp.where(upper, SUB - 1 - m, m) for m in range(HALO)]

        def plane(i, p, m):
            start = side * (flat[i].shape[0] // 2) + p * lev * SUB + sub[m]
            return flat[i][pl.ds(start, lev, stride=SUB), :]

        for m in range(HALO):
            for p in range(2):
                out[AT_T + 2 * m + p] = plane(0, p, m)
        for at, i, count in ((AT_E, 1, N_E), (AT_N, 2, N_N), (AT_K, 3, N_K)):
            for m in range(count):
                out[at + m] = plane(i, 0, m)
        out[AT_WET] = jnp.zeros((lev, cols), jnp.float32)
        for m in range(N_K):
            out[AT_WET, pl.ds(m, 1), :] = wets[pl.ds(side * SUB + sub[m], 1), :].astype(jnp.float32)


def fill_kernel(tr, ec, nc, kd, wet, te, ee, ne, ke, ce, wets, done):
    rows, cols = wet.shape
    lev = ec.shape[0]
    copies = [(wet, wets)]
    for source, target in ((kd, ke), (tr, te), (ec, ee), (nc, ne)):
        copies.append((source, target.at[:, pl.ds(SUB, rows), :]))
    copies = [pltpu.make_async_copy(a, b, done.at[i]) for i, (a, b) in enumerate(copies)]
    for copy in copies:
        copy.start()
    zero = jnp.zeros((SUB, cols), jnp.float32)

    def clear(p):
        for start in (0, SUB + rows):
            for target in (ee, ne, ke):
                target[p, pl.ds(start, SUB), :] = zero
            te[p, pl.ds(start, SUB), :] = zero
            te[p + lev, pl.ds(start, SUB), :] = zero

    loop(lev, clear)
    for start in (0, SUB + rows):
        ce[pl.ds(start, SUB), :] = zero
    for copy in copies:
        copy.wait()
    ce[pl.ds(SUB, rows), :] = wets[...].astype(jnp.float32)

    def dry(p):
        for b in range(rows // SUB):
            at = pl.ds(SUB + b * SUB, SUB)
            wet_cells = wets[pl.ds(b * SUB, SUB), :] > p
            ke[p, at, :] = jnp.where(wet_cells, ke[p, at, :], -1.0)

    loop(lev, dry)


def turn_kernel(te_in, ee_in, ne_in, ke_in, ce_in, x, y, te, ee, ne, ke, ce, t0, sp, kh, p0, p1, cw):
    planes, tall, cols = te.shape
    lev = ee.shape[0]
    te, ee, ne, ke = (ref.reshape(ref.shape[0] * tall, cols) for ref in (te, ee, ne, ke))
    lon_even, lat_even, top = parities()
    bottom = lax.axis_index("lat") == 0
    shape = (lev, cols)
    lane = lanes(shape)
    level = lax.broadcasted_iota(jnp.int32, shape, 0).astype(jnp.float32)
    zero = jnp.zeros((SUB, cols), jnp.float32)
    turn = jnp.where(top, -1.0, 1.0)
    cells = jnp.where(top, cols - 1 - lane, lane)
    faces = jnp.where(top, jnp.where(lane == cols - 1, cols - 1, cols - 2 - lane), lane)
    for north in (False, True):
        def piece(at):
            a, b = x[at], y[at]
            if north:
                return jnp.where(lat_even, a, b)
            return jnp.where(bottom, 0.0, jnp.where(lat_even, b, a))

        def put(target, row, value, first=0):
            target[pl.ds(first * tall + row, lev, stride=tall), :] = value

        def turned(value, index):
            return take(value, index) if north else value

        at = [tall - SUB + m if north else SUB - 1 - m for m in range(HALO)]
        for m in range(HALO):
            for i in range(2):
                put(te, at[m], turned(piece(AT_T + 2 * m + i), cells), i * lev)
        wets = piece(AT_WET)
        for m in range(N_K):
            counts = jnp.broadcast_to(wets[m : m + 1], shape)
            kappa = jnp.where(level < counts, piece(AT_K + m), -1.0)
            put(ke, at[m], turned(kappa, cells))
        wets = turned(wets, cells)
        for m in range(N_K):
            ce[pl.ds(at[m], 1), :] = wets[m : m + 1]
        for m in range(N_E):
            value = turned(piece(AT_E + m), faces)
            put(ee, at[m], turn * value if north else value)
        if north:
            speeds = [turn * take(piece(AT_N + m), cells) for m in range(N_N)]
            last = ne[pl.ds(tall - SUB - 1, lev, stride=tall), :]
            put(ne, tall - SUB - 1, jnp.where(top, 0.5 * (last + speeds[0]), last))
            for m in range(N_E):
                put(ne, at[m], jnp.where(top, speeds[m + 1], speeds[m]))
        else:
            for m in range(N_N):
                put(ne, at[m], piece(AT_N + m))

    def rows_of(source, j, n):
        return [source[pl.ds(p * tall + j, tall // SUB, stride=SUB), :] for p in range(n)]

    def transpose(i):
        for k in range(SUB // 4):
            j = i * (SUB // 4) + k
            for row in (2 * j, 2 * j + 1):
                t0[row, pl.ds(SUB, cols), :] = jnp.concatenate(rows_of(te, row, planes), 0).T
                both = rows_of(ee, row, lev) + rows_of(ne, row, lev)
                sp[row, pl.ds(SUB, cols), :] = jnp.concatenate(both, 0).T
            both = rows_of(ke, j, lev) + rows_of(ke, j + SUB // 2, lev)
            kh[j, pl.ds(SUB, cols), :] = jnp.concatenate(both, 0).T

    loop(2, transpose)
    for j in range(SUB):
        sp[j, pl.ds(SUB - 1, 1), :] = sp[j, pl.ds(SUB + cols - 1, 1), :]

    parts = [ce[pl.ds(j, tall // SUB, stride=SUB), :] for j in range(SUB)]
    cw[pl.ds(SUB, cols), :] = jnp.concatenate(parts * (cols // tall), 0).T

    left = lanes((SUB, cols)) < cols // 2
    for out, eastern in ((p0, lon_even), (p1, jnp.logical_not(lon_even))):
        out[0:SUB, :] = zero
        far = pl.ds(jnp.where(eastern, SUB + cols - HALO, SUB), SUB)
        here = pl.ds(jnp.where(eastern, SUB + cols - FEW, SUB), SUB)
        faced = pl.ds(jnp.where(eastern, SUB + cols - FEW, SUB - 1), SUB)
        for j in range(SUB):
            out[pl.ds(SPARE + j * HALO, SUB), :] = t0[j, far, :]
        for j in range(SUB):
            out[pl.ds(SPARE + AT_SPEED + j * FEW, SUB), :] = jnp.where(left, sp[j, faced, :], sp[j, here, :])
        for j in range(SUB // 2):
            out[pl.ds(SPARE + AT_KAPPA + j * FEW, SUB), :] = jnp.maximum(kh[j, here, :], 0.0)
        out[pl.ds(SPARE + AT_COUNT, SUB), :] = cw[here, :]


def coefficients(speed, kappa, other_kappa):
    wet = jnp.minimum(kappa, other_kappa) > 0
    speed = jnp.where(wet, speed, 0.0)
    magnitude = jnp.abs(speed)
    spread = jnp.minimum(speed, 0.0) - jnp.where(wet, 0.5 * (kappa + other_kappa), 0.0)
    return speed, spread, 0.5 * magnitude * (1.0 - magnitude)


def all_coefficients(se, sn, kw, face, low, at, kappa_low, kappa_high, north_low):
    here = pl.ds(at, SUB)
    kappa = [kw[j, here, :] for j in range(SUB)] + [kappa_high]
    for c, value in enumerate(coefficients(north_low, kappa_low, kappa[0])):
        low[c, here, :] = value
    for j in range(SUB):
        eastern = coefficients(se[j, here, :], kappa[j], kw[j, pl.ds(at + 1, SUB), :])
        northern = coefficients(sn[j, here, :], kappa[j], kappa[j + 1])
        for c, value in enumerate(eastern + northern):
            face[c, j, here, :] = value


def flux(cell, before, here, after, face):
    speed, spread, slope = face
    upslope = jnp.where(speed > 0, before, after)
    limited = jnp.maximum(
        jnp.minimum(here, upslope), jnp.minimum(jnp.maximum(here, upslope), 0.0)
    )
    return speed * cell + spread * here + slope * limited


def east_flux(t, face, s, j, at):
    behind, cell, after, beyond = (t[s, j, pl.ds(at + i, SUB), :] for i in (-1, 0, 1, 2))
    coefs = tuple(face[c, j, pl.ds(at, SUB), :] for c in range(3))
    return flux(cell, cell - behind, after - cell, beyond - after, coefs)


def advance(t, face, low, s, at, beside, fluxes, kept=None):
    here = pl.ds(at, SUB)
    cell = [t[s, j, here, :] for j in range(SUB)]
    east = [east_flux(t, face, s, j, at) for j in range(SUB)]
    for j in range(SUB):
        fluxes[j, here, :] = east[j]
    divergence = [east[j] - fluxes[j, pl.ds(at - 1, SUB), :] for j in range(SUB)]
    rows = [beside[0], beside[1], *cell, beside[2], beside[3]]
    slope = [b - a for a, b in zip(rows, rows[1:])]
    north = []
    for j in range(-1, SUB):
        coefs = tuple(low[c, here, :] if j < 0 else face[3 + c, j, here, :] for c in range(3))
        north.append(flux(rows[j + 2], slope[j + 1], slope[j + 2], slope[j + 3], coefs))
    for j in range(SUB):
        value = cell[j] - divergence[j] - (north[j + 1] - north[j])
        t[s + 1, j, here, :] = value if kept is None else jnp.where(kept, t[s + 1, j, here, :], value)


def rows_beside(t, s, at):
    here = pl.ds(at, SUB)
    before = [earlier_block(t[s, j, here, :]) for j in (SUB - 2, SUB - 1)]
    return before + [later_block(t[s, j, here, :]) for j in (0, 1)]


def interior_kernel(t0, sp, kh, t, face, low, se, sn, kw, fluxes, beside):
    cols = t.shape[3]
    passes = cols // SUB // PAIR

    def start(g):
        return pl.multiple_of(SUB + g * SUB, SUB)

    lane = lanes((SUB, cols))
    half = cols // 2
    left = lane < half
    within = lane & (half - 1)
    before = half + ((within - 1) & (half - 1))
    after = (within + 1) & (half - 1)

    def halves(value):
        other = pltpu.roll(value, half, 1)
        return jnp.where(left, value, other), jnp.where(left, other, value)

    def turn_coefficients(b):
        values = []
        for k in range(PAIR):
            here = pl.ds(start(b * PAIR + k), SUB)
            values.append((
                take(kh[SUB // 2 - 1, here, :], before), take(kh[0, here, :], after), take(sp[SUB - 1, here, :], before)
            ))
        return values

    def spread(b):
        values = []
        for k in range(PAIR):
            here = pl.ds(start(b * PAIR + k), SUB)
            speeds = [halves(sp[j, here, :]) for j in range(SUB)]
            values.append((here, speeds, [halves(kh[j, here, :]) for j in range(SUB // 2)]))
        return values

    def put_spread(values):
        for here, speeds, kappas in values:
            for j, (eastern, northern) in enumerate(speeds):
                se[j, here, :], sn[j, here, :] = eastern, northern
            for j, (lower, upper) in enumerate(kappas):
                kw[j, here, :], kw[j + SUB // 2, here, :] = lower, upper

    def turn_cells(n):
        s = lax.div(n, passes)
        return [rows_beside(t, s, start((n - s * passes) * PAIR + k)) for k in range(PAIR)]

    def keep(values):
        for k, group in enumerate(values):
            for i, value in enumerate(group):
                beside[k, i] = value

    def prepare(n):
        b = jnp.maximum(n - 1, 0)
        turned = [[beside[k, i] for i in range(3)] for k in range(PAIR)]
        following = jnp.minimum(n, passes - 1)
        later = turn_coefficients(following)
        values = spread(following)
        for k in range(PAIR):
            if k == PAIR - 1:
                put_spread(values)
            at = start(b * PAIR + k)
            for j in range(SUB):
                t[0, j, pl.ds(at, SUB), :] = t0[j, pl.ds(at, SUB), :]
            all_coefficients(se, sn, kw, face, low, at, *turned[k])
        keep(later)

    wrapped = [halves(sp[j, 0:SUB, :])[0] for j in range(SUB)]
    loop(passes + 1, prepare)
    for j in range(SUB):
        se[j, 0:SUB, :] = wrapped[j]
    keep(turn_cells(0))

    def step(n):
        turned = [[beside[k, i] for i in range(4)] for k in range(PAIR)]
        s = lax.div(n, passes)
        later = turn_cells(jnp.minimum(n + 1, STEPS * passes - 1))
        for k in range(PAIR):
            advance(t, face, low, s, start((n - s * passes) * PAIR + k), turned[k], fluxes)
        keep(later)

    loop(STEPS * passes, step)


def frame_kernel(t_in, face_in, se_in, sn_in, kw_in, low_in, r0, r1, out, t, face, se, sn, kw, low, tall, fluxes, done):
    cols = t.shape[3]
    planes, rows = out.shape[:2]
    height = tall.shape[0] // planes
    lon_even, _, top = parities()
    shape = (SUB, cols)
    lane = lanes(shape)
    sub = lax.broadcasted_iota(jnp.int32, shape, 0)
    left = lane < cols // 2
    blocks = height // SUB
    block = lane & (blocks - 1)
    level = (lax.shift_right_logical(lane, blocks.bit_length() - 1)) & (planes // 2 - 1)
    level = level.astype(jnp.float32)
    fold = top & (block == blocks - 1)
    end = SUB + cols

    def halves(value):
        other = pltpu.roll(value, cols // 2, 1)
        return jnp.where(left, value, other), jnp.where(left, other, value)

    for west in (False, True):
        def piece(at, n):
            rows_at = pl.ds(SPARE + at - (SUB - n if west else 0), SUB)
            a, b = r0[rows_at, :], r1[rows_at, :]
            return jnp.where(lon_even, b, a) if west else jnp.where(lon_even, a, b)

        here = pl.ds(0 if west else end, SUB)
        faced = here if west else pl.ds(end - 1, SUB)
        kept = (sub == SUB - 1) & fold if west else (sub == 0) & jnp.logical_not(fold)
        counts = piece(AT_COUNT, FEW)
        for j in range(SUB):
            t[0, j, here, :] = piece(j * HALO, HALO)
            speed, northern = halves(piece(AT_SPEED + j * FEW, FEW))
            sn[j, here, :] = northern
            se[j, faced, :] = jnp.where(kept, se[j, faced, :], speed)
        for j in range(SUB // 2):
            for row, kappa in zip((j, j + SUB // 2), halves(piece(AT_KAPPA + j * FEW, FEW))):
                wet = level < take(counts, block + row * blocks)
                kw[row, here, :] = jnp.where(wet, kappa, -1.0)
    for at in (0, end - 1):
        here = pl.ds(at, SUB)
        all_coefficients(
            se, sn, kw, face, low, at,
            earlier_block(kw[SUB - 1, here, :]), later_block(kw[0, here, :]), earlier_block(sn[SUB - 1, here, :]),
        )

    def step(s):
        west = SUB - 2 * (STEPS - 1) + 2 * s - 1
        east = end - SUB + 2 * (STEPS - 1) - 2 * s
        beside = [rows_beside(t, s, at) for at in (west, east)]
        advance(t, face, low, s, west, beside[0], fluxes)
        advance(t, face, low, s, east, beside[1], fluxes, sub == 0)

    for s in range(STEPS):
        step(s)

    def transpose(i):
        n = height // SUB
        for k in range(SUB):
            j = SUB * i + k
            matrix = t[STEPS, j, pl.ds(SUB, cols), :].T
            for p in range(planes):
                tall[pl.ds(p * height + j, n, stride=SUB), :] = matrix[p * n : (p + 1) * n]

    transpose(0)
    copy = pltpu.make_async_copy(
        tall.reshape(planes, height, cols).at[:, pl.ds(SUB, rows), :], out, done
    )
    copy.start()
    copy.wait()


def call(kernel, shapes, *operands, specs=None, outs=None, grant=SMALL, scratch=(), alias=None):
    return pl.pallas_call(
        kernel,
        out_shape=[jax.ShapeDtypeStruct(s, jnp.float32) for s in shapes],
        in_specs=specs or [VMEM] * len(operands),
        out_specs=outs or [VMEM] * len(shapes),
        scratch_shapes=[pltpu.VMEM(s, jnp.float32) if isinstance(s, tuple) else s for s in scratch],
        input_output_aliases=alias or {},
        compiler_params=pltpu.CompilerParams(vmem_limit_bytes=grant),
        cost_estimate=pl.CostEstimate(flops=1 << 20, bytes_accessed=1 << 20, transcendentals=0),
    )(*operands)


def lon_swap(sizes, parity):
    lon, lat = sizes
    pairs = []
    for i in range(lon):
        other = (i + 1 if i % 2 == parity else i - 1) % lon
        pairs += [(i * lat + j, other * lat + j) for j in range(lat)]
    return pairs


def lat_swap(sizes, parity):
    lon, lat = sizes
    pairs = []
    for i in range(lon):
        for j in range(lat):
            if j % 2 != parity:
                other = (i, j - 1) if j > 0 else (i ^ 1, j)
            else:
                other = (i, j + 1) if j + 1 < lat else (lon - 1 - i, j)
            pairs.append((i * lat + j, other[0] * lat + other[1]))
    return pairs


def per_device(tracers, east_courant, north_courant, diffusivity, wet_levels):
    count, lev, rows, cols = tracers.shape
    planes, tall = count * lev, rows + 2 * SUB
    blocks = tall // SUB
    assert planes * blocks == cols and rows % SUB == 0
    assert blocks & (blocks - 1) == 0 and lev & (lev - 1) == 0 and blocks == lev == SUB
    sizes = (lax.axis_size("lon"), lax.axis_size("lat"))
    message = (MESSAGE, lev, cols)
    given = [
        pltpu.with_memory_space_constraint(v, pltpu.HBM)
        for v in (tracers.reshape(planes, rows, cols), east_courant, north_courant, diffusivity, wet_levels)
    ]
    x, y = call(
        edge_kernel, [message] * 2, *given, specs=[ANY] * 5,
        scratch=[(2 * n, SUB, cols) for n in (planes, lev, lev, lev)]
        + [pltpu.VMEM((2 * SUB, cols), jnp.int32), pltpu.SemaphoreType.DMA((10,))],
    )
    y = lax.ppermute(y, AXES, lat_swap(sizes, 1))
    x = lax.ppermute(x, AXES, lat_swap(sizes, 0))
    extended = [(n, tall, cols) for n in (planes, lev, lev, lev)] + [(tall, cols)]
    filled = call(
        fill_kernel, extended, *given, specs=[ANY] * 5,
        scratch=[pltpu.VMEM((rows, cols), jnp.int32), pltpu.SemaphoreType.DMA((5,))],
    )
    wide = (SUB, cols + 2 * SUB, cols)
    packed = (COLUMNS, cols)
    *_, t0, sp, kh, p0, p1 = call(
        turn_kernel, extended + [wide] * 2 + [(SUB // 2,) + wide[1:]] + [packed] * 2, *filled, x, y, alias={i: i for i in range(5)},
        scratch=[wide[1:]],
    )
    r1 = lax.ppermute(p1, AXES, lon_swap(sizes, 1))
    r0 = lax.ppermute(p0, AXES, lon_swap(sizes, 0))
    t, face, low, se, sn, kw = call(
        interior_kernel, [(STEPS + 1,) + wide, (6,) + wide, (3,) + wide[1:]] + [wide] * 3, t0, sp, kh,
        scratch=[wide, (PAIR, 4, SUB, cols)],
    )
    out, *_ = call(
        frame_kernel, [(planes, rows, cols), t.shape, face.shape, wide, wide, wide, low.shape],
        t, face, se, sn, kw, low, r0, r1,
        outs=[ANY] + [VMEM] * 6, alias={i: i + 1 for i in range(6)},
        scratch=[(planes * tall, cols), wide, pltpu.SemaphoreType.DMA],
    )
    return out.reshape(tracers.shape)


def solution(mesh):
    placed = (
        P(None, None, "lat", "lon"),
        P(None, "lat", "lon"),
        P(None, "lat", "lon"),
        P(None, "lat", "lon"),
        P("lat", "lon"),
    )
    return jax.shard_map(
        per_device,
        mesh=mesh,
        in_specs=placed,
        out_specs=P(None, None, "lat", "lon"),
        check_vma=False,
    )
```

```python
import jax
import jax.numpy as jnp
from jax import lax
from jax.experimental import pallas as pl
from jax.experimental.pallas import tpu as pltpu
from jax.sharding import PartitionSpec as P


STEPS = 3
HALO = 2 * STEPS
AXES = ("lon", "lat")
SUB = 8
FEW = HALO - 1
AT_SPEED, AT_KAPPA = SUB * HALO, SUB * HALO + SUB * FEW
AT_COUNT = AT_KAPPA + SUB // 2 * FEW
SPARE = 2
PAIR = 8
COLUMNS = -(-(SPARE + AT_COUNT + SUB) // SUB) * SUB
SMALL = 16 << 20
VMEM = pl.BlockSpec(memory_space=pltpu.VMEM)
ANY = pl.BlockSpec(memory_space=pl.ANY)

AT_T, AT_E, AT_N, AT_K, AT_WET, MESSAGE = 0, 12, 16, 21, 26, 27
N_E, N_N, N_K = HALO - 2, HALO - 1, HALO - 1


def lanes(shape):
    return lax.broadcasted_iota(jnp.int32, shape, len(shape) - 1)


def take(value, index):
    return jnp.take_along_axis(value, index, axis=1)


def later_block(value):
    return pltpu.roll(value, value.shape[1] - 1, 1)


def earlier_block(value):
    return pltpu.roll(value, 1, 1)


def loop(count, body):
    def step(i, _):
        body(i)
        return 0

    lax.fori_loop(0, count, step, 0)


def parities():
    lon_even = lax.rem(lax.axis_index("lon"), 2) == 0
    lat = lax.axis_index("lat")
    return lon_even, lax.rem(lat, 2) == 0, lat == lax.axis_size("lat") - 1


def edge_kernel(tr, ec, nc, kd, wet, x, y, trs, ecs, ncs, kds, wets, done):
    rows, cols = wet.shape
    lev = ec.shape[0]
    _, lat_even, _ = parities()
    copies = []
    for side, start in enumerate((0, rows - SUB)):
        for source, target in ((tr, trs), (ec, ecs), (nc, ncs), (kd, kds)):
            n = source.shape[0]
            copies.append((source.at[:, pl.ds(start, SUB), :], target.at[pl.ds(side * n, n)]))
        copies.append((wet.at[pl.ds(start, SUB), :], wets.at[pl.ds(side * SUB, SUB), :]))
    copies = [pltpu.make_async_copy(a, b, done.at[i]) for i, (a, b) in enumerate(copies)]
    for copy in copies:
        copy.start()
    for copy in copies:
        copy.wait()
    flat = [ref.reshape(ref.shape[0] * SUB, cols) for ref in (trs, ecs, ncs, kds)]
    for out, upper in ((x, lat_even), (y, jnp.logical_not(lat_even))):
        side = jnp.where(upper, 1, 0)
        sub = [jnp.where(upper, SUB - 1 - m, m) for m in range(HALO)]

        def plane(i, p, m):
            start = side * (flat[i].shape[0] // 2) + p * lev * SUB + sub[m]
            return flat[i][pl.ds(start, lev, stride=SUB), :]

        for m in range(HALO):
            for p in range(2):
                out[AT_T + 2 * m + p] = plane(0, p, m)
        for at, i, count in ((AT_E, 1, N_E), (AT_N, 2, N_N), (AT_K, 3, N_K)):
            for m in range(count):
                out[at + m] = plane(i, 0, m)
        out[AT_WET] = jnp.zeros((lev, cols), jnp.float32)
        for m in range(N_K):
            out[AT_WET, pl.ds(m, 1), :] = wets[pl.ds(side * SUB + sub[m], 1), :].astype(jnp.float32)


def fill_kernel(tr, ec, nc, kd, wet, te, ee, ne, ke, ce, wets, done):
    rows, cols = wet.shape
    lev = ec.shape[0]
    copies = [(wet, wets)]
    for source, target in ((kd, ke), (tr, te), (ec, ee), (nc, ne)):
        copies.append((source, target.at[:, pl.ds(SUB, rows), :]))
    copies = [pltpu.make_async_copy(a, b, done.at[i]) for i, (a, b) in enumerate(copies)]
    for copy in copies:
        copy.start()
    zero = jnp.zeros((SUB, cols), jnp.float32)

    def clear(p):
        for start in (0, SUB + rows):
            for target in (ee, ne, ke):
                target[p, pl.ds(start, SUB), :] = zero
            te[p, pl.ds(start, SUB), :] = zero
            te[p + lev, pl.ds(start, SUB), :] = zero

    loop(lev, clear)
    for start in (0, SUB + rows):
        ce[pl.ds(start, SUB), :] = zero
    for copy in copies:
        copy.wait()
    ce[pl.ds(SUB, rows), :] = wets[...].astype(jnp.float32)

    def dry(p):
        for b in range(rows // SUB):
            at = pl.ds(SUB + b * SUB, SUB)
            wet_cells = wets[pl.ds(b * SUB, SUB), :] > p
            ke[p, at, :] = jnp.where(wet_cells, ke[p, at, :], -1.0)

    loop(lev, dry)


def turn_kernel(te_in, ee_in, ne_in, ke_in, ce_in, x, y, te, ee, ne, ke, ce, t0, sp, kh, p0, p1, cw):
    planes, tall, cols = te.shape
    lev = ee.shape[0]
    te, ee, ne, ke = (ref.reshape(ref.shape[0] * tall, cols) for ref in (te, ee, ne, ke))
    lon_even, lat_even, top = parities()
    bottom = lax.axis_index("lat") == 0
    shape = (lev, cols)
    lane = lanes(shape)
    level = lax.broadcasted_iota(jnp.int32, shape, 0).astype(jnp.float32)
    zero = jnp.zeros((SUB, cols), jnp.float32)
    turn = jnp.where(top, -1.0, 1.0)
    cells = jnp.where(top, cols - 1 - lane, lane)
    faces = jnp.where(top, jnp.where(lane == cols - 1, cols - 1, cols - 2 - lane), lane)
    for north in (False, True):
        def piece(at):
            a, b = x[at], y[at]
            if north:
                return jnp.where(lat_even, a, b)
            return jnp.where(bottom, 0.0, jnp.where(lat_even, b, a))

        def put(target, row, value, first=0):
            target[pl.ds(first * tall + row, lev, stride=tall), :] = value

        def turned(value, index):
            return take(value, index) if north else value

        at = [tall - SUB + m if north else SUB - 1 - m for m in range(HALO)]
        for m in range(HALO):
            for i in range(2):
                put(te, at[m], turned(piece(AT_T + 2 * m + i), cells), i * lev)
        wets = piece(AT_WET)
        for m in range(N_K):
            counts = jnp.broadcast_to(wets[m : m + 1], shape)
            kappa = jnp.where(level < counts, piece(AT_K + m), -1.0)
            put(ke, at[m], turned(kappa, cells))
        wets = turned(wets, cells)
        for m in range(N_K):
            ce[pl.ds(at[m], 1), :] = wets[m : m + 1]
        for m in range(N_E):
            value = turned(piece(AT_E + m), faces)
            put(ee, at[m], turn * value if north else value)
        if north:
            speeds = [turn * take(piece(AT_N + m), cells) for m in range(N_N)]
            last = ne[pl.ds(tall - SUB - 1, lev, stride=tall), :]
            put(ne, tall - SUB - 1, jnp.where(top, 0.5 * (last + speeds[0]), last))
            for m in range(N_E):
                put(ne, at[m], jnp.where(top, speeds[m + 1], speeds[m]))
        else:
            for m in range(N_N):
                put(ne, at[m], piece(AT_N + m))

    def rows_of(source, j, n):
        return [source[pl.ds(p * tall + j, tall // SUB, stride=SUB), :] for p in range(n)]

    def transpose(i):
        for k in range(SUB // 4):
            j = i * (SUB // 4) + k
            for row in (2 * j, 2 * j + 1):
                t0[row, pl.ds(SUB, cols), :] = jnp.concatenate(rows_of(te, row, planes), 0).T
                both = rows_of(ee, row, lev) + rows_of(ne, row, lev)
                sp[row, pl.ds(SUB, cols), :] = jnp.concatenate(both, 0).T
            both = rows_of(ke, j, lev) + rows_of(ke, j + SUB // 2, lev)
            kh[j, pl.ds(SUB, cols), :] = jnp.concatenate(both, 0).T

    loop(2, transpose)
    for j in range(SUB):
        sp[j, pl.ds(SUB - 1, 1), :] = sp[j, pl.ds(SUB + cols - 1, 1), :]

    parts = [ce[pl.ds(j, tall // SUB, stride=SUB), :] for j in range(SUB)]
    cw[pl.ds(SUB, cols), :] = jnp.concatenate(parts * (cols // tall), 0).T

    left = lanes((SUB, cols)) < cols // 2
    for out, eastern in ((p0, lon_even), (p1, jnp.logical_not(lon_even))):
        out[0:SUB, :] = zero
        far = pl.ds(jnp.where(eastern, SUB + cols - HALO, SUB), SUB)
        here = pl.ds(jnp.where(eastern, SUB + cols - FEW, SUB), SUB)
        faced = pl.ds(jnp.where(eastern, SUB + cols - FEW, SUB - 1), SUB)
        for j in range(SUB):
            out[pl.ds(SPARE + j * HALO, SUB), :] = t0[j, far, :]
        for j in range(SUB):
            out[pl.ds(SPARE + AT_SPEED + j * FEW, SUB), :] = jnp.where(left, sp[j, faced, :], sp[j, here, :])
        for j in range(SUB // 2):
            out[pl.ds(SPARE + AT_KAPPA + j * FEW, SUB), :] = jnp.maximum(kh[j, here, :], 0.0)
        out[pl.ds(SPARE + AT_COUNT, SUB), :] = cw[here, :]


def coefficients(speed, kappa, other_kappa):
    wet = jnp.minimum(kappa, other_kappa) > 0
    speed = jnp.where(wet, speed, 0.0)
    magnitude = jnp.abs(speed)
    spread = jnp.minimum(speed, 0.0) - jnp.where(wet, 0.5 * (kappa + other_kappa), 0.0)
    return speed, spread, 0.5 * magnitude * (1.0 - magnitude)


def all_coefficients(se, sn, kw, face, low, at, kappa_low, kappa_high, north_low):
    here = pl.ds(at, SUB)
    kappa = [kw[j, here, :] for j in range(SUB)] + [kappa_high]
    for c, value in enumerate(coefficients(north_low, kappa_low, kappa[0])):
        low[c, here, :] = value
    for j in range(SUB):
        eastern = coefficients(se[j, here, :], kappa[j], kw[j, pl.ds(at + 1, SUB), :])
        northern = coefficients(sn[j, here, :], kappa[j], kappa[j + 1])
        for c, value in enumerate(eastern + northern):
            face[c, j, here, :] = value


def flux(cell, before, here, after, face):
    speed, spread, slope = face
    upslope = jnp.where(speed > 0, before, after)
    limited = jnp.maximum(
        jnp.minimum(here, upslope), jnp.minimum(jnp.maximum(here, upslope), 0.0)
    )
    return speed * cell + spread * here + slope * limited


def east_flux(t, face, s, j, at):
    behind, cell, after, beyond = (t[s, j, pl.ds(at + i, SUB), :] for i in (-1, 0, 1, 2))
    coefs = tuple(face[c, j, pl.ds(at, SUB), :] for c in range(3))
    return flux(cell, cell - behind, after - cell, beyond - after, coefs)


def advance(t, face, low, s, at, beside, fluxes, kept=None):
    here = pl.ds(at, SUB)
    cell = [t[s, j, here, :] for j in range(SUB)]
    east = [east_flux(t, face, s, j, at) for j in range(SUB)]
    for j in range(SUB):
        fluxes[j, here, :] = east[j]
    divergence = [east[j] - fluxes[j, pl.ds(at - 1, SUB), :] for j in range(SUB)]
    rows = [beside[0], beside[1], *cell, beside[2], beside[3]]
    slope = [b - a for a, b in zip(rows, rows[1:])]
    north = []
    for j in range(-1, SUB):
        coefs = tuple(low[c, here, :] if j < 0 else face[3 + c, j, here, :] for c in range(3))
        north.append(flux(rows[j + 2], slope[j + 1], slope[j + 2], slope[j + 3], coefs))
    for j in range(SUB):
        value = cell[j] - divergence[j] - (north[j + 1] - north[j])
        t[s + 1, j, here, :] = value if kept is None else jnp.where(kept, t[s + 1, j, here, :], value)


def rows_beside(t, s, at):
    here = pl.ds(at, SUB)
    before = [earlier_block(t[s, j, here, :]) for j in (SUB - 2, SUB - 1)]
    return before + [later_block(t[s, j, here, :]) for j in (0, 1)]


def interior_kernel(t0, sp, kh, t, face, low, se, sn, kw, fluxes, beside):
    cols = t.shape[3]
    passes = cols // SUB // PAIR

    def start(g):
        return pl.multiple_of(SUB + g * SUB, SUB)

    lane = lanes((SUB, cols))
    half = cols // 2
    left = lane < half
    within = lane & (half - 1)
    before = half + ((within - 1) & (half - 1))
    after = (within + 1) & (half - 1)

    def halves(value):
        other = pltpu.roll(value, half, 1)
        return jnp.where(left, value, other), jnp.where(left, other, value)

    def turn_coefficients(b):
        values = []
        for k in range(PAIR):
            here = pl.ds(start(b * PAIR + k), SUB)
            values.append((
                take(kh[SUB // 2 - 1, here, :], before), take(kh[0, here, :], after), take(sp[SUB - 1, here, :], before)
            ))
        return values

    def spread(b):
        values = []
        for k in range(PAIR):
            here = pl.ds(start(b * PAIR + k), SUB)
            speeds = [halves(sp[j, here, :]) for j in range(SUB)]
            values.append((here, speeds, [halves(kh[j, here, :]) for j in range(SUB // 2)]))
        return values

    def put_spread(values):
        for here, speeds, kappas in values:
            for j, (eastern, northern) in enumerate(speeds):
                se[j, here, :], sn[j, here, :] = eastern, northern
            for j, (lower, upper) in enumerate(kappas):
                kw[j, here, :], kw[j + SUB // 2, here, :] = lower, upper

    def turn_cells(n):
        s = lax.div(n, passes)
        return [rows_beside(t, s, start((n - s * passes) * PAIR + k)) for k in range(PAIR)]

    def keep(values):
        for k, group in enumerate(values):
            for i, value in enumerate(group):
                beside[k, i] = value

    def prepare(n, more=True):
        b = jnp.maximum(n - 1, 0)
        turned = [[beside[k, i] for i in range(3)] for k in range(PAIR)]
        if more:
            later = turn_coefficients(n)
            values = spread(n)
        for k in range(PAIR):
            if more and k == PAIR - 1:
                put_spread(values)
            at = start(b * PAIR + k)
            for j in range(SUB):
                t[0, j, pl.ds(at, SUB), :] = t0[j, pl.ds(at, SUB), :]
            all_coefficients(se, sn, kw, face, low, at, *turned[k])
        if more:
            keep(later)

    wrapped = [halves(sp[j, 0:SUB, :])[0] for j in range(SUB)]
    loop(passes, prepare)
    prepare(passes, False)
    for j in range(SUB):
        se[j, 0:SUB, :] = wrapped[j]
    keep(turn_cells(0))

    def step(n):
        turned = [[beside[k, i] for i in range(4)] for k in range(PAIR)]
        s = lax.div(n, passes)
        later = turn_cells(jnp.minimum(n + 1, STEPS * passes - 1))
        for k in range(PAIR):
            advance(t, face, low, s, start((n - s * passes) * PAIR + k), turned[k], fluxes)
        keep(later)

    loop(STEPS * passes, step)


def frame_kernel(t_in, face_in, se_in, sn_in, kw_in, low_in, r0, r1, out, t, face, se, sn, kw, low, tall, fluxes, done):
    cols = t.shape[3]
    planes, rows = out.shape[:2]
    height = tall.shape[0] // planes
    lon_even, _, top = parities()
    shape = (SUB, cols)
    lane = lanes(shape)
    sub = lax.broadcasted_iota(jnp.int32, shape, 0)
    left = lane < cols // 2
    blocks = height // SUB
    block = lane & (blocks - 1)
    level = (lax.shift_right_logical(lane, blocks.bit_length() - 1)) & (planes // 2 - 1)
    level = level.astype(jnp.float32)
    fold = top & (block == blocks - 1)
    end = SUB + cols

    def halves(value):
        other = pltpu.roll(value, cols // 2, 1)
        return jnp.where(left, value, other), jnp.where(left, other, value)

    for west in (False, True):
        def piece(at, n):
            rows_at = pl.ds(SPARE + at - (SUB - n if west else 0), SUB)
            a, b = r0[rows_at, :], r1[rows_at, :]
            return jnp.where(lon_even, b, a) if west else jnp.where(lon_even, a, b)

        here = pl.ds(0 if west else end, SUB)
        faced = here if west else pl.ds(end - 1, SUB)
        kept = (sub == SUB - 1) & fold if west else (sub == 0) & jnp.logical_not(fold)
        counts = piece(AT_COUNT, FEW)
        for j in range(SUB):
            t[0, j, here, :] = piece(j * HALO, HALO)
            speed, northern = halves(piece(AT_SPEED + j * FEW, FEW))
            sn[j, here, :] = northern
            se[j, faced, :] = jnp.where(kept, se[j, faced, :], speed)
        for j in range(SUB // 2):
            for row, kappa in zip((j, j + SUB // 2), halves(piece(AT_KAPPA + j * FEW, FEW))):
                wet = level < take(counts, block + row * blocks)
                kw[row, here, :] = jnp.where(wet, kappa, -1.0)
    for at in (0, end - 1):
        here = pl.ds(at, SUB)
        all_coefficients(
            se, sn, kw, face, low, at,
            earlier_block(kw[SUB - 1, here, :]), later_block(kw[0, here, :]), earlier_block(sn[SUB - 1, here, :]),
        )

    def step(s):
        west = SUB - 2 * (STEPS - 1) + 2 * s - 1
        east = end - SUB + 2 * (STEPS - 1) - 2 * s
        beside = [rows_beside(t, s, at) for at in (west, east)]
        advance(t, face, low, s, west, beside[0], fluxes)
        advance(t, face, low, s, east, beside[1], fluxes, sub == 0)

    for s in range(STEPS):
        step(s)

    def transpose(i):
        n = height // SUB
        for k in range(SUB):
            j = SUB * i + k
            matrix = t[STEPS, j, pl.ds(SUB, cols), :].T
            for p in range(planes):
                tall[pl.ds(p * height + j, n, stride=SUB), :] = matrix[p * n : (p + 1) * n]

    transpose(0)
    copy = pltpu.make_async_copy(
        tall.reshape(planes, height, cols).at[:, pl.ds(SUB, rows), :], out, done
    )
    copy.start()
    copy.wait()


def call(kernel, shapes, *operands, specs=None, outs=None, grant=SMALL, scratch=(), alias=None):
    return pl.pallas_call(
        kernel,
        out_shape=[jax.ShapeDtypeStruct(s, jnp.float32) for s in shapes],
        in_specs=specs or [VMEM] * len(operands),
        out_specs=outs or [VMEM] * len(shapes),
        scratch_shapes=[pltpu.VMEM(s, jnp.float32) if isinstance(s, tuple) else s for s in scratch],
        input_output_aliases=alias or {},
        compiler_params=pltpu.CompilerParams(vmem_limit_bytes=grant),
        cost_estimate=pl.CostEstimate(flops=1 << 20, bytes_accessed=1 << 20, transcendentals=0),
    )(*operands)


def lon_swap(sizes, parity):
    lon, lat = sizes
    pairs = []
    for i in range(lon):
        other = (i + 1 if i % 2 == parity else i - 1) % lon
        pairs += [(i * lat + j, other * lat + j) for j in range(lat)]
    return pairs


def lat_swap(sizes, parity):
    lon, lat = sizes
    pairs = []
    for i in range(lon):
        for j in range(lat):
            if j % 2 != parity:
                other = (i, j - 1) if j > 0 else (i ^ 1, j)
            else:
                other = (i, j + 1) if j + 1 < lat else (lon - 1 - i, j)
            pairs.append((i * lat + j, other[0] * lat + other[1]))
    return pairs


def per_device(tracers, east_courant, north_courant, diffusivity, wet_levels):
    count, lev, rows, cols = tracers.shape
    planes, tall = count * lev, rows + 2 * SUB
    blocks = tall // SUB
    assert planes * blocks == cols and rows % SUB == 0
    assert blocks & (blocks - 1) == 0 and lev & (lev - 1) == 0 and blocks == lev == SUB
    sizes = (lax.axis_size("lon"), lax.axis_size("lat"))
    message = (MESSAGE, lev, cols)
    given = [
        pltpu.with_memory_space_constraint(v, pltpu.HBM)
        for v in (tracers.reshape(planes, rows, cols), east_courant, north_courant, diffusivity, wet_levels)
    ]
    x, y = call(
        edge_kernel, [message] * 2, *given, specs=[ANY] * 5,
        scratch=[(2 * n, SUB, cols) for n in (planes, lev, lev, lev)]
        + [pltpu.VMEM((2 * SUB, cols), jnp.int32), pltpu.SemaphoreType.DMA((10,))],
    )
    y = lax.ppermute(y, AXES, lat_swap(sizes, 1))
    x = lax.ppermute(x, AXES, lat_swap(sizes, 0))
    extended = [(n, tall, cols) for n in (planes, lev, lev, lev)] + [(tall, cols)]
    filled = call(
        fill_kernel, extended, *given, specs=[ANY] * 5,
        scratch=[pltpu.VMEM((rows, cols), jnp.int32), pltpu.SemaphoreType.DMA((5,))],
    )
    wide = (SUB, cols + 2 * SUB, cols)
    packed = (COLUMNS, cols)
    *_, t0, sp, kh, p0, p1 = call(
        turn_kernel, extended + [wide] * 2 + [(SUB // 2,) + wide[1:]] + [packed] * 2, *filled, x, y, alias={i: i for i in range(5)},
        scratch=[wide[1:]],
    )
    r1 = lax.ppermute(p1, AXES, lon_swap(sizes, 1))
    r0 = lax.ppermute(p0, AXES, lon_swap(sizes, 0))
    t, face, low, se, sn, kw = call(
        interior_kernel, [(STEPS + 1,) + wide, (6,) + wide, (3,) + wide[1:]] + [wide] * 3, t0, sp, kh,
        scratch=[wide, (PAIR, 4, SUB, cols)],
    )
    out, *_ = call(
        frame_kernel, [(planes, rows, cols), t.shape, face.shape, wide, wide, wide, low.shape],
        t, face, se, sn, kw, low, r0, r1,
        outs=[ANY] + [VMEM] * 6, alias={i: i + 1 for i in range(6)},
        scratch=[(planes * tall, cols), wide, pltpu.SemaphoreType.DMA],
    )
    return out.reshape(tracers.shape)


def solution(mesh):
    placed = (
        P(None, None, "lat", "lon"),
        P(None, "lat", "lon"),
        P(None, "lat", "lon"),
        P(None, "lat", "lon"),
        P("lat", "lon"),
    )
    return jax.shard_map(
        per_device,
        mesh=mesh,
        in_specs=placed,
        out_specs=P(None, None, "lat", "lon"),
        check_vma=False,
    )
```

```python
import jax
import jax.numpy as jnp
from jax import lax
from jax.experimental import pallas as pl
from jax.experimental.pallas import tpu as pltpu
from jax.sharding import PartitionSpec as P


STEPS = 3
HALO = 2 * STEPS
AXES = ("lon", "lat")
SUB = 8
FEW = HALO - 1
AT_SPEED, AT_KAPPA = SUB * HALO, SUB * HALO + SUB * FEW
AT_COUNT = AT_KAPPA + SUB // 2 * FEW
SPARE = 2
DRY = -1e9
PAIR = 8
COLUMNS = -(-(SPARE + AT_COUNT + SUB) // SUB) * SUB
SMALL = 16 << 20
VMEM = pl.BlockSpec(memory_space=pltpu.VMEM)
ANY = pl.BlockSpec(memory_space=pl.ANY)

AT_T, AT_E, AT_N, AT_K, AT_WET, MESSAGE = 0, 12, 16, 21, 26, 27
N_E, N_N, N_K = HALO - 2, HALO - 1, HALO - 1


def lanes(shape):
    return lax.broadcasted_iota(jnp.int32, shape, len(shape) - 1)


def take(value, index):
    return jnp.take_along_axis(value, index, axis=1)


def later_block(value):
    return pltpu.roll(value, value.shape[1] - 1, 1)


def earlier_block(value):
    return pltpu.roll(value, 1, 1)


def loop(count, body):
    def step(i, _):
        body(i)
        return 0

    lax.fori_loop(0, count, step, 0)


def parities():
    lon_even = lax.rem(lax.axis_index("lon"), 2) == 0
    lat = lax.axis_index("lat")
    return lon_even, lax.rem(lat, 2) == 0, lat == lax.axis_size("lat") - 1


def edge_kernel(tr, ec, nc, kd, wet, x, y, trs, ecs, ncs, kds, wets, done):
    rows, cols = wet.shape
    lev = ec.shape[0]
    _, lat_even, _ = parities()
    copies = []
    for side, start in enumerate((0, rows - SUB)):
        for source, target in ((tr, trs), (ec, ecs), (nc, ncs), (kd, kds)):
            n = source.shape[0]
            copies.append((source.at[:, pl.ds(start, SUB), :], target.at[pl.ds(side * n, n)]))
        copies.append((wet.at[pl.ds(start, SUB), :], wets.at[pl.ds(side * SUB, SUB), :]))
    copies = [pltpu.make_async_copy(a, b, done.at[i]) for i, (a, b) in enumerate(copies)]
    for copy in copies:
        copy.start()
    for copy in copies:
        copy.wait()
    flat = [ref.reshape(ref.shape[0] * SUB, cols) for ref in (trs, ecs, ncs, kds)]
    for out, upper in ((x, lat_even), (y, jnp.logical_not(lat_even))):
        side = jnp.where(upper, 1, 0)
        sub = [jnp.where(upper, SUB - 1 - m, m) for m in range(HALO)]

        def plane(i, p, m):
            start = side * (flat[i].shape[0] // 2) + p * lev * SUB + sub[m]
            return flat[i][pl.ds(start, lev, stride=SUB), :]

        for m in range(HALO):
            for p in range(2):
                out[AT_T + 2 * m + p] = plane(0, p, m)
        for at, i, count in ((AT_E, 1, N_E), (AT_N, 2, N_N), (AT_K, 3, N_K)):
            for m in range(count):
                out[at + m] = plane(i, 0, m)
        out[AT_WET] = jnp.zeros((lev, cols), jnp.float32)
        for m in range(N_K):
            out[AT_WET, pl.ds(m, 1), :] = wets[pl.ds(side * SUB + sub[m], 1), :].astype(jnp.float32)


def fill_kernel(tr, ec, nc, kd, wet, te, ee, ne, ke, ce, wets, done):
    rows, cols = wet.shape
    lev = ec.shape[0]
    copies = [(wet, wets)]
    for source, target in ((kd, ke), (tr, te), (ec, ee), (nc, ne)):
        copies.append((source, target.at[:, pl.ds(SUB, rows), :]))
    copies = [pltpu.make_async_copy(a, b, done.at[i]) for i, (a, b) in enumerate(copies)]
    for copy in copies:
        copy.start()
    zero = jnp.zeros((SUB, cols), jnp.float32)

    def clear(p):
        for start in (0, SUB + rows):
            for target in (ee, ne, ke):
                target[p, pl.ds(start, SUB), :] = zero
            te[p, pl.ds(start, SUB), :] = zero
            te[p + lev, pl.ds(start, SUB), :] = zero

    loop(lev, clear)
    for start in (0, SUB + rows):
        ce[pl.ds(start, SUB), :] = zero
    for copy in copies:
        copy.wait()
    ce[pl.ds(SUB, rows), :] = wets[...].astype(jnp.float32)

    def dry(p):
        for b in range(rows // SUB):
            at = pl.ds(SUB + b * SUB, SUB)
            wet_cells = wets[pl.ds(b * SUB, SUB), :] > p
            ke[p, at, :] = jnp.where(wet_cells, 0.5 * ke[p, at, :], DRY)

    loop(lev, dry)


def turn_kernel(te_in, ee_in, ne_in, ke_in, ce_in, x, y, te, ee, ne, ke, ce, t0, sp, kh, p0, p1, cw):
    planes, tall, cols = te.shape
    lev = ee.shape[0]
    te, ee, ne, ke = (ref.reshape(ref.shape[0] * tall, cols) for ref in (te, ee, ne, ke))
    lon_even, lat_even, top = parities()
    bottom = lax.axis_index("lat") == 0
    shape = (lev, cols)
    lane = lanes(shape)
    level = lax.broadcasted_iota(jnp.int32, shape, 0).astype(jnp.float32)
    zero = jnp.zeros((SUB, cols), jnp.float32)
    turn = jnp.where(top, -1.0, 1.0)
    cells = jnp.where(top, cols - 1 - lane, lane)
    faces = jnp.where(top, jnp.where(lane == cols - 1, cols - 1, cols - 2 - lane), lane)
    for north in (False, True):
        def piece(at):
            a, b = x[at], y[at]
            if north:
                return jnp.where(lat_even, a, b)
            return jnp.where(bottom, 0.0, jnp.where(lat_even, b, a))

        def put(target, row, value, first=0):
            target[pl.ds(first * tall + row, lev, stride=tall), :] = value

        def turned(value, index):
            return take(value, index) if north else value

        at = [tall - SUB + m if north else SUB - 1 - m for m in range(HALO)]
        for m in range(HALO):
            for i in range(2):
                put(te, at[m], turned(piece(AT_T + 2 * m + i), cells), i * lev)
        wets = piece(AT_WET)
        for m in range(N_K):
            counts = jnp.broadcast_to(wets[m : m + 1], shape)
            kappa = jnp.where(level < counts, 0.5 * piece(AT_K + m), DRY)
            put(ke, at[m], turned(kappa, cells))
        wets = turned(wets, cells)
        for m in range(N_K):
            ce[pl.ds(at[m], 1), :] = wets[m : m + 1]
        for m in range(N_E):
            value = turned(piece(AT_E + m), faces)
            put(ee, at[m], turn * value if north else value)
        if north:
            speeds = [turn * take(piece(AT_N + m), cells) for m in range(N_N)]
            last = ne[pl.ds(tall - SUB - 1, lev, stride=tall), :]
            put(ne, tall - SUB - 1, jnp.where(top, 0.5 * (last + speeds[0]), last))
            for m in range(N_E):
                put(ne, at[m], jnp.where(top, speeds[m + 1], speeds[m]))
        else:
            for m in range(N_N):
                put(ne, at[m], piece(AT_N + m))

    def rows_of(source, j, n):
        return [source[pl.ds(p * tall + j, tall // SUB, stride=SUB), :] for p in range(n)]

    def transpose(i):
        for k in range(SUB // 4):
            j = i * (SUB // 4) + k
            for row in (2 * j, 2 * j + 1):
                t0[row, pl.ds(SUB, cols), :] = jnp.concatenate(rows_of(te, row, planes), 0).T
                both = rows_of(ee, row, lev) + rows_of(ne, row, lev)
                sp[row, pl.ds(SUB, cols), :] = jnp.concatenate(both, 0).T
            both = rows_of(ke, j, lev) + rows_of(ke, j + SUB // 2, lev)
            kh[j, pl.ds(SUB, cols), :] = jnp.concatenate(both, 0).T

    loop(2, transpose)
    for j in range(SUB):
        sp[j, pl.ds(SUB - 1, 1), :] = sp[j, pl.ds(SUB + cols - 1, 1), :]

    parts = [ce[pl.ds(j, tall // SUB, stride=SUB), :] for j in range(SUB)]
    cw[pl.ds(SUB, cols), :] = jnp.concatenate(parts * (cols // tall), 0).T

    left = lanes((SUB, cols)) < cols // 2
    for out, eastern in ((p0, lon_even), (p1, jnp.logical_not(lon_even))):
        out[0:SUB, :] = zero
        far = pl.ds(jnp.where(eastern, SUB + cols - HALO, SUB), SUB)
        here = pl.ds(jnp.where(eastern, SUB + cols - FEW, SUB), SUB)
        faced = pl.ds(jnp.where(eastern, SUB + cols - FEW, SUB - 1), SUB)
        for j in range(SUB):
            out[pl.ds(SPARE + j * HALO, SUB), :] = t0[j, far, :]
        for j in range(SUB):
            out[pl.ds(SPARE + AT_SPEED + j * FEW, SUB), :] = jnp.where(left, sp[j, faced, :], sp[j, here, :])
        for j in range(SUB // 2):
            out[pl.ds(SPARE + AT_KAPPA + j * FEW, SUB), :] = jnp.maximum(kh[j, here, :], 0.0)
        out[pl.ds(SPARE + AT_COUNT, SUB), :] = cw[here, :]


def coefficients(speed, kappa, other_kappa):
    face_kappa = kappa + other_kappa
    speed = jnp.where(face_kappa > 0, speed, 0.0)
    magnitude = jnp.abs(speed)
    spread = jnp.minimum(speed, 0.0) - jnp.maximum(face_kappa, 0.0)
    return speed, spread, magnitude * (0.5 - 0.5 * magnitude)


def all_coefficients(se, sn, kw, face, low, at, kappa_low, kappa_high, north_low):
    here = pl.ds(at, SUB)
    kappa = [kw[j, here, :] for j in range(SUB)] + [kappa_high]
    for c, value in enumerate(coefficients(north_low, kappa_low, kappa[0])):
        low[c, here, :] = value
    for j in range(SUB):
        eastern = coefficients(se[j, here, :], kappa[j], kw[j, pl.ds(at + 1, SUB), :])
        northern = coefficients(sn[j, here, :], kappa[j], kappa[j + 1])
        for c, value in enumerate(eastern + northern):
            face[c, j, here, :] = value


def flux(cell, before, here, after, face):
    speed, spread, slope = face
    upslope = jnp.where(speed > 0, before, after)
    limited = jnp.maximum(
        jnp.minimum(here, upslope), jnp.minimum(jnp.maximum(here, upslope), 0.0)
    )
    return speed * cell + spread * here + slope * limited


def east_flux(t, face, s, j, at):
    behind, cell, after, beyond = (t[s, j, pl.ds(at + i, SUB), :] for i in (-1, 0, 1, 2))
    coefs = tuple(face[c, j, pl.ds(at, SUB), :] for c in range(3))
    return flux(cell, cell - behind, after - cell, beyond - after, coefs)


def advance(t, face, low, s, at, beside, fluxes, kept=None):
    here = pl.ds(at, SUB)
    cell = [t[s, j, here, :] for j in range(SUB)]
    east = [east_flux(t, face, s, j, at) for j in range(SUB)]
    for j in range(SUB):
        fluxes[j, here, :] = east[j]
    divergence = [east[j] - fluxes[j, pl.ds(at - 1, SUB), :] for j in range(SUB)]
    rows = [beside[0], beside[1], *cell, beside[2], beside[3]]
    slope = [b - a for a, b in zip(rows, rows[1:])]
    north = []
    for j in range(-1, SUB):
        coefs = tuple(low[c, here, :] if j < 0 else face[3 + c, j, here, :] for c in range(3))
        north.append(flux(rows[j + 2], slope[j + 1], slope[j + 2], slope[j + 3], coefs))
    for j in range(SUB):
        value = cell[j] - divergence[j] - (north[j + 1] - north[j])
        t[s + 1, j, here, :] = value if kept is None else jnp.where(kept, t[s + 1, j, here, :], value)


def rows_beside(t, s, at):
    here = pl.ds(at, SUB)
    before = [earlier_block(t[s, j, here, :]) for j in (SUB - 2, SUB - 1)]
    return before + [later_block(t[s, j, here, :]) for j in (0, 1)]


def interior_kernel(t0, sp, kh, t, face, low, se, sn, kw, fluxes, beside):
    cols = t.shape[3]
    passes = cols // SUB // PAIR

    def start(g):
        return pl.multiple_of(SUB + g * SUB, SUB)

    lane = lanes((SUB, cols))
    half = cols // 2
    left = lane < half
    within = lane & (half - 1)
    before = half + ((within - 1) & (half - 1))
    after = (within + 1) & (half - 1)

    def halves(value):
        other = pltpu.roll(value, half, 1)
        return jnp.where(left, value, other), jnp.where(left, other, value)

    def turn_coefficients(b):
        values = []
        for k in range(PAIR):
            here = pl.ds(start(b * PAIR + k), SUB)
            values.append((
                take(kh[SUB // 2 - 1, here, :], before), take(kh[0, here, :], after), take(sp[SUB - 1, here, :], before)
            ))
        return values

    def spread(b):
        values = []
        for k in range(PAIR):
            here = pl.ds(start(b * PAIR + k), SUB)
            speeds = [halves(sp[j, here, :]) for j in range(SUB)]
            values.append((here, speeds, [halves(kh[j, here, :]) for j in range(SUB // 2)]))
        return values

    def put_spread(values):
        for here, speeds, kappas in values:
            for j, (eastern, northern) in enumerate(speeds):
                se[j, here, :], sn[j, here, :] = eastern, northern
            for j, (lower, upper) in enumerate(kappas):
                kw[j, here, :], kw[j + SUB // 2, here, :] = lower, upper

    def turn_cells(n):
        s = lax.div(n, passes)
        return [rows_beside(t, s, start((n - s * passes) * PAIR + k)) for k in range(PAIR)]

    def keep(values):
        for k, group in enumerate(values):
            for i, value in enumerate(group):
                beside[k, i] = value

    def prepare(n, more=True):
        b = jnp.maximum(n - 1, 0)
        turned = [[beside[k, i] for i in range(3)] for k in range(PAIR)]
        if more:
            later = turn_coefficients(n)
            values = spread(n)
        for k in range(PAIR):
            if more and k == PAIR - 1:
                put_spread(values)
            at = start(b * PAIR + k)
            for j in range(SUB):
                t[0, j, pl.ds(at, SUB), :] = t0[j, pl.ds(at, SUB), :]
            all_coefficients(se, sn, kw, face, low, at, *turned[k])
        if more:
            keep(later)

    wrapped = [halves(sp[j, 0:SUB, :])[0] for j in range(SUB)]
    loop(passes, prepare)
    prepare(passes, False)
    for j in range(SUB):
        se[j, 0:SUB, :] = wrapped[j]
    keep(turn_cells(0))

    def step(n):
        turned = [[beside[k, i] for i in range(4)] for k in range(PAIR)]
        s = lax.div(n, passes)
        later = turn_cells(jnp.minimum(n + 1, STEPS * passes - 1))
        for k in range(PAIR):
            advance(t, face, low, s, start((n - s * passes) * PAIR + k), turned[k], fluxes)
        keep(later)

    loop(STEPS * passes, step)


def frame_kernel(t_in, face_in, se_in, sn_in, kw_in, low_in, r0, r1, out, t, face, se, sn, kw, low, tall, fluxes, done):
    cols = t.shape[3]
    planes, rows = out.shape[:2]
    height = tall.shape[0] // planes
    lon_even, _, top = parities()
    shape = (SUB, cols)
    lane = lanes(shape)
    sub = lax.broadcasted_iota(jnp.int32, shape, 0)
    left = lane < cols // 2
    blocks = height // SUB
    block = lane & (blocks - 1)
    level = (lax.shift_right_logical(lane, blocks.bit_length() - 1)) & (planes // 2 - 1)
    level = level.astype(jnp.float32)
    fold = top & (block == blocks - 1)
    end = SUB + cols

    def halves(value):
        other = pltpu.roll(value, cols // 2, 1)
        return jnp.where(left, value, other), jnp.where(left, other, value)

    for west in (False, True):
        def piece(at, n):
            rows_at = pl.ds(SPARE + at - (SUB - n if west else 0), SUB)
            a, b = r0[rows_at, :], r1[rows_at, :]
            return jnp.where(lon_even, b, a) if west else jnp.where(lon_even, a, b)

        here = pl.ds(0 if west else end, SUB)
        faced = here if west else pl.ds(end - 1, SUB)
        kept = (sub == SUB - 1) & fold if west else (sub == 0) & jnp.logical_not(fold)
        counts = piece(AT_COUNT, FEW)
        for j in range(SUB):
            t[0, j, here, :] = piece(j * HALO, HALO)
            speed, northern = halves(piece(AT_SPEED + j * FEW, FEW))
            sn[j, here, :] = northern
            se[j, faced, :] = jnp.where(kept, se[j, faced, :], speed)
        for j in range(SUB // 2):
            for row, kappa in zip((j, j + SUB // 2), halves(piece(AT_KAPPA + j * FEW, FEW))):
                wet = level < take(counts, block + row * blocks)
                kw[row, here, :] = jnp.where(wet, kappa, DRY)
    for at in (0, end - 1):
        here = pl.ds(at, SUB)
        all_coefficients(
            se, sn, kw, face, low, at,
            earlier_block(kw[SUB - 1, here, :]), later_block(kw[0, here, :]), earlier_block(sn[SUB - 1, here, :]),
        )

    def step(s):
        west = SUB - 2 * (STEPS - 1) + 2 * s - 1
        east = end - SUB + 2 * (STEPS - 1) - 2 * s
        beside = [rows_beside(t, s, at) for at in (west, east)]
        advance(t, face, low, s, west, beside[0], fluxes)
        advance(t, face, low, s, east, beside[1], fluxes, sub == 0)

    for s in range(STEPS):
        step(s)

    def transpose(i):
        n = height // SUB
        for k in range(SUB):
            j = SUB * i + k
            matrix = t[STEPS, j, pl.ds(SUB, cols), :].T
            for p in range(planes):
                tall[pl.ds(p * height + j, n, stride=SUB), :] = matrix[p * n : (p + 1) * n]

    transpose(0)
    copy = pltpu.make_async_copy(
        tall.reshape(planes, height, cols).at[:, pl.ds(SUB, rows), :], out, done
    )
    copy.start()
    copy.wait()


def call(kernel, shapes, *operands, specs=None, outs=None, grant=SMALL, scratch=(), alias=None):
    return pl.pallas_call(
        kernel,
        out_shape=[jax.ShapeDtypeStruct(s, jnp.float32) for s in shapes],
        in_specs=specs or [VMEM] * len(operands),
        out_specs=outs or [VMEM] * len(shapes),
        scratch_shapes=[pltpu.VMEM(s, jnp.float32) if isinstance(s, tuple) else s for s in scratch],
        input_output_aliases=alias or {},
        compiler_params=pltpu.CompilerParams(vmem_limit_bytes=grant),
        cost_estimate=pl.CostEstimate(flops=1 << 20, bytes_accessed=1 << 20, transcendentals=0),
    )(*operands)


def lon_swap(sizes, parity):
    lon, lat = sizes
    pairs = []
    for i in range(lon):
        other = (i + 1 if i % 2 == parity else i - 1) % lon
        pairs += [(i * lat + j, other * lat + j) for j in range(lat)]
    return pairs


def lat_swap(sizes, parity):
    lon, lat = sizes
    pairs = []
    for i in range(lon):
        for j in range(lat):
            if j % 2 != parity:
                other = (i, j - 1) if j > 0 else (i ^ 1, j)
            else:
                other = (i, j + 1) if j + 1 < lat else (lon - 1 - i, j)
            pairs.append((i * lat + j, other[0] * lat + other[1]))
    return pairs


def per_device(tracers, east_courant, north_courant, diffusivity, wet_levels):
    count, lev, rows, cols = tracers.shape
    planes, tall = count * lev, rows + 2 * SUB
    blocks = tall // SUB
    assert planes * blocks == cols and rows % SUB == 0
    assert blocks & (blocks - 1) == 0 and lev & (lev - 1) == 0 and blocks == lev == SUB
    sizes = (lax.axis_size("lon"), lax.axis_size("lat"))
    message = (MESSAGE, lev, cols)
    given = [
        pltpu.with_memory_space_constraint(v, pltpu.HBM)
        for v in (tracers.reshape(planes, rows, cols), east_courant, north_courant, diffusivity, wet_levels)
    ]
    x, y = call(
        edge_kernel, [message] * 2, *given, specs=[ANY] * 5,
        scratch=[(2 * n, SUB, cols) for n in (planes, lev, lev, lev)]
        + [pltpu.VMEM((2 * SUB, cols), jnp.int32), pltpu.SemaphoreType.DMA((10,))],
    )
    y = lax.ppermute(y, AXES, lat_swap(sizes, 1))
    x = lax.ppermute(x, AXES, lat_swap(sizes, 0))
    extended = [(n, tall, cols) for n in (planes, lev, lev, lev)] + [(tall, cols)]
    filled = call(
        fill_kernel, extended, *given, specs=[ANY] * 5,
        scratch=[pltpu.VMEM((rows, cols), jnp.int32), pltpu.SemaphoreType.DMA((5,))],
    )
    wide = (SUB, cols + 2 * SUB, cols)
    packed = (COLUMNS, cols)
    *_, t0, sp, kh, p0, p1 = call(
        turn_kernel, extended + [wide] * 2 + [(SUB // 2,) + wide[1:]] + [packed] * 2, *filled, x, y, alias={i: i for i in range(5)},
        scratch=[wide[1:]],
    )
    r1 = lax.ppermute(p1, AXES, lon_swap(sizes, 1))
    r0 = lax.ppermute(p0, AXES, lon_swap(sizes, 0))
    t, face, low, se, sn, kw = call(
        interior_kernel, [(STEPS + 1,) + wide, (6,) + wide, (3,) + wide[1:]] + [wide] * 3, t0, sp, kh,
        scratch=[wide, (PAIR, 4, SUB, cols)],
    )
    out, *_ = call(
        frame_kernel, [(planes, rows, cols), t.shape, face.shape, wide, wide, wide, low.shape],
        t, face, se, sn, kw, low, r0, r1,
        outs=[ANY] + [VMEM] * 6, alias={i: i + 1 for i in range(6)},
        scratch=[(planes * tall, cols), wide, pltpu.SemaphoreType.DMA],
    )
    return out.reshape(tracers.shape)


def solution(mesh):
    placed = (
        P(None, None, "lat", "lon"),
        P(None, "lat", "lon"),
        P(None, "lat", "lon"),
        P(None, "lat", "lon"),
        P("lat", "lon"),
    )
    return jax.shard_map(
        per_device,
        mesh=mesh,
        in_specs=placed,
        out_specs=P(None, None, "lat", "lon"),
        check_vma=False,
    )
```
